256 devices in a mesh: ctx: 64 (over y, z, core), head: 4 (over x).
Axes of the slice: x: 4, y: 4, z: 8, core: 2. Of those that a mesh axis runs over, the one named last changes fastest.
Arguments:
- lin_query: bfloat16 [8192, 6144], P('ctx', 'head'), may hold values from -6 to 6
- lin_key: bfloat16 [8192, 6144], P('ctx', 'head'), may hold values from -6 to 6
- lin_value: bfloat16 [8192, 6144], P('ctx', 'head'), may hold values from -6 to 6
- soft_query: bfloat16 [8192, 6144], P('ctx', 'head'), may hold values from -6 to 6
- soft_key: bfloat16 [8192, 6144], P('ctx', 'head'), may hold values from -6 to 6
- soft_value: bfloat16 [8192, 6144], P('ctx', 'head'), may hold values from -6 to 6
- upstream: bfloat16 [8192, 6144], P('ctx', 'head'), may hold values from -6 to 6
- doc_lengths: int32 [42], replicated, may hold values from 1 to 384, 8192 in all
- doc_domain: int32 [42], replicated, may hold values from 0 to 7
- domain_weight: float32 [8], replicated, may hold values from 0.25 to 4
Outputs:
- lin_dq: bfloat16 [8192, 6144], P('ctx', 'head')
- lin_dk: bfloat16 [8192, 6144], P('ctx', 'head')
- lin_dv: bfloat16 [8192, 6144], P('ctx', 'head')
- soft_dq: bfloat16 [8192, 6144], P('ctx', 'head')
- soft_dk: bfloat16 [8192, 6144], P('ctx', 'head')
- soft_dv: bfloat16 [8192, 6144], P('ctx', 'head')
- domain_loss: float32 [8], replicated
The draws below stay inside these ranges and needn't reach their ends.
Inputs may be any that keep to these rules, and one draw needn't show every extreme that they name: `doc_lengths`: whole documents fill the sequence in order; the longest has exactly 384 tokens.
All inputs are finite; a program needn't handle non-finite values.
Results may differ from the reference program's by a relative error of at most 0.029.
Values may be sent and summed in bfloat16 or wider, within the bound.
No kernel may reach another device: no remote copies, remote signals or barrier semaphores. Data moves between devices by JAX's collectives and lax.ppermute only.
A program may use at most 192 MiB of HBM per device.

```python
import math
import jax
import jax.numpy as jnp
import numpy as np
from jax import lax

HEADS = 48
HD = 128
TOK_DEV = 128
REACH = 3
NDOM = 8
SEQ = 8192
DOC_MOST = 384
NDOCS = 42
N_CTX = 64


def soft_pair(key):
    base = jax.random.fold_in(key, 11)
    first_key, second_key = jax.random.split(base, 2)
    shape = (SEQ, HEADS * HD)
    queries = jnp.clip(jax.random.normal(first_key, shape, jnp.float32), -6.0, 6.0)
    keyset = jnp.clip(jax.random.normal(second_key, shape, jnp.float32), -6.0, 6.0)
    return (queries, keyset)


def draw_soft_query(key, part):
    queries, keyset = soft_pair(key)
    return queries.astype(jnp.bfloat16)


def draw_soft_key(key, part):
    queries, keyset = soft_pair(key)
    return keyset.astype(jnp.bfloat16)


def place_ends(entries, rng, least, largest):
    dims = entries.shape
    index_at = [jax.random.randint(jax.random.fold_in(rng, axis), (), 0, dims[axis]) for axis in range(len(dims))]
    entries = entries.at[tuple(index_at)].set(least)
    longest = dims.index(max(dims))
    index_at[longest] = (index_at[longest] + 1) % dims[longest]
    return entries.at[tuple(index_at)].set(largest)


def steps_of(own_key, dims, cuts, smallest, largest):
    def one(position, parts):
        draws = jax.random.uniform(jax.random.fold_in(jax.random.fold_in(own_key, 6), position), (parts,), jnp.float32, smallest / len(cuts), largest / len(cuts))
        return jnp.repeat(jnp.exp(draws), dims[position] // parts).reshape((-1,) + (1,) * (len(dims) - position - 1))

    level = one(*cuts[0])
    for cut in cuts[1:]:
        level = level * one(*cut)
    return level


def split_up(amount, total, limit, slope):
    weights = [(1 << 20) // math.isqrt(rank ** slope) + 1 for rank in range(2, amount + 1)]
    rest, given = total - limit - (amount - 1), [1] * (amount - 1)
    while rest > 0:
        movable = [i for i in range(amount - 1) if given[i] < limit]
        pool, left = sum([weights[i] for i in movable]), rest
        for i in movable:
            more = min(limit - given[i], max(1, left * weights[i] // pool), rest)
            given[i] = given[i] + more
            rest = rest - more
    return np.array([limit] + given)


def ragged_sizes(own_key, amount, total, limit, slope):
    if amount == 2:
        one = jax.random.randint(own_key, (), max(1, total - limit), min(limit, total - 1) + 1)
        return jnp.stack([one, total - one])
    sizes = jnp.asarray(split_up(amount, total, limit, slope), jnp.int32)
    twos = (amount - 1) // 2
    source_of, taker = sizes[1:1 + 2 * twos:2], sizes[2:2 + 2 * twos:2]
    margin = jnp.minimum(source_of - 1, limit - taker)
    passed = jax.random.randint(jax.random.fold_in(own_key, 1), (twos,), 0, 1 << 20) % (margin + 1)
    sizes = sizes.at[1:1 + 2 * twos:2].set(source_of - passed).at[2:2 + 2 * twos:2].set(taker + passed)
    return sizes[jax.random.permutation(jax.random.fold_in(own_key, 2), amount)]


def gaussian(key, dims, spread, limit, cuts=(), held_as=jnp.bfloat16):
    entries = jax.random.normal(key, dims, jnp.float32) * spread
    if len(cuts) > 0:
        entries = steps_of(key, dims, cuts, -0.22, 0.18) * entries
    return jnp.clip(entries, min=-limit, max=limit).astype(held_as)


def setup_inputs(seed: int = 0) -> dict:
    streams_of = jax.random.split(jax.random.key(seed), 11)
    lin_query = gaussian(streams_of[0], (SEQ, HEADS * HD), 1.0, 6.0, ((0, 64), (1, 4)))
    lin_key = gaussian(streams_of[1], (SEQ, HEADS * HD), 1.0, 6.0, ((0, 64), (1, 4)))
    lin_value = gaussian(streams_of[2], (SEQ, HEADS * HD), 1.0, 6.0, ((0, 64), (1, 4)))
    soft_query = draw_soft_query(jax.random.fold_in(streams_of[10], 71), 0)
    soft_key = draw_soft_key(jax.random.fold_in(streams_of[10], 71), 0)
    soft_value = gaussian(streams_of[5], (SEQ, HEADS * HD), 1.0, 6.0, ((0, 64), (1, 4)))
    upstream = gaussian(streams_of[6], (SEQ, HEADS * HD), 1.0, 6.0, ((0, 64), (1, 4)))
    doc_lengths = ragged_sizes(streams_of[7], NDOCS, SEQ, DOC_MOST, 2).astype(jnp.int32)
    doc_domain = place_ends(jax.random.randint(streams_of[8], (NDOCS,), 0, NDOM), jax.random.fold_in(streams_of[8], 1), 0, NDOM - 1).astype(jnp.int32)
    domain_weight = jnp.clip(jnp.exp(jax.random.uniform(streams_of[9], (NDOM,), jnp.float32, math.log(0.25), math.log(4.0))), 0.25, 4.0)
    return {"lin_query": lin_query, "lin_key": lin_key, "lin_value": lin_value, "soft_query": soft_query, "soft_key": soft_key, "soft_value": soft_value, "upstream": upstream, "doc_lengths": doc_lengths, "doc_domain": doc_domain, "domain_weight": domain_weight}


def token_docs(doc_lengths, positions):
    doc_ends = jnp.cumsum(doc_lengths).astype(jnp.int32)
    doc_starts = (doc_ends - doc_lengths).astype(jnp.int32)
    inside = (doc_starts[None, :] <= positions[:, None]) & (positions[:, None] < doc_ends[None, :])
    numbers = jnp.arange(1, doc_lengths.shape[0] + 1, dtype=jnp.int32)
    doc_index = (jnp.sum(jnp.where(inside, numbers[None, :], 0), axis=1) - 1).astype(jnp.int32)
    doc_begin = jnp.sum(jnp.where(inside, doc_starts[None, :], 0), axis=1).astype(jnp.int32)
    doc_finish = jnp.sum(jnp.where(inside, doc_ends[None, :], 0), axis=1).astype(jnp.int32)
    return inside, doc_index, doc_begin, doc_finish


def token_weights(inside, doc_domain, domain_weight):
    domain_of = jnp.sum(jnp.where(inside, doc_domain[None, :], 0), axis=1).astype(jnp.int32)
    domain_ids = jnp.arange(domain_weight.shape[0], dtype=jnp.int32)
    domain_hot = (domain_of[:, None] == domain_ids[None, :]).astype(jnp.float32)
    return jnp.sum(domain_hot * domain_weight[None, :], axis=1), domain_hot


def reference(lin_query, lin_key, lin_value, soft_query, soft_key, soft_value, upstream, doc_lengths, doc_domain, domain_weight):
    feat_cols = HEADS * HD
    linear_scale = (HD * DOC_MOST) ** -0.5
    soft_scale = HD ** -0.5
    highest_index = lax.Precision.HIGHEST
    positions = jnp.arange(SEQ, dtype=jnp.int32)
    inside, doc_index, doc_begin, doc_finish = token_docs(doc_lengths, positions)
    weights, domain_hot = token_weights(inside, doc_domain, domain_weight)
    grad_out = (weights[:, None] * upstream.astype(jnp.float32)).astype(jnp.bfloat16)

    def blocked(array):
        return array.reshape(N_CTX, TOK_DEV, HEADS, HD)

    query_b, key_b, value_b, grad_b = blocked(lin_query), blocked(lin_key), blocked(lin_value), blocked(grad_out)
    index_b = doc_index.reshape(N_CTX, TOK_DEV)
    begin_b = doc_begin.reshape(N_CTX, TOK_DEV)
    finish_b = doc_finish.reshape(N_CTX, TOK_DEV)
    block_ids = jnp.arange(N_CTX, dtype=jnp.int32)
    order = jnp.arange(TOK_DEV, dtype=jnp.int32)

    def local_scores(query_rows, key_rows, value_rows, gradient_heads, ids):
        allowed = (ids[:, None] == ids[None, :]) & (order[None, :] <= order[:, None])
        lin_scores = jnp.where(allowed[None], linear_scale * jnp.einsum('thd,shd->hts', query_rows.astype(jnp.float32), key_rows.astype(jnp.float32)), 0.0).astype(jnp.bfloat16)
        lin_back = jnp.where(allowed[None], linear_scale * jnp.einsum('thd,shd->hts', gradient_heads.astype(jnp.float32), value_rows.astype(jnp.float32)), 0.0).astype(jnp.bfloat16)
        return lin_scores, lin_back

    def forward_step(summed_state, inputs):
        query_rows, key_rows, value_rows, gradient_heads, ids, begins, block = inputs
        row_start = block * TOK_DEV
        lin_scores, lin_back = local_scores(query_rows, key_rows, value_rows, gradient_heads, ids)
        carried_along = (begins < row_start).astype(jnp.float32)[:, None, None]
        inner = jnp.einsum('hts,shd->thd', lin_scores.astype(jnp.float32), value_rows.astype(jnp.float32))
        outer_product = linear_scale * carried_along * jnp.einsum('jlb,lbw->jlw', query_rows.astype(jnp.float32), summed_state, precision=highest_index)
        lin_out = (inner + outer_product).astype(jnp.bfloat16)
        dq_inner = jnp.einsum('hts,shd->thd', lin_back.astype(jnp.float32), key_rows.astype(jnp.float32))
        outer_query_gradient = linear_scale * carried_along * jnp.einsum('nmu,meu->nme', gradient_heads.astype(jnp.float32), summed_state, precision=highest_index)
        lin_dq = (dq_inner + outer_query_gradient).astype(jnp.bfloat16)
        last_onehot = (ids == ids[TOK_DEV - 1]).astype(jnp.float32)[:, None, None]
        local_state = jnp.einsum('lzd,lzj->zdj', key_rows.astype(jnp.float32) * last_onehot, value_rows.astype(jnp.float32))
        flag = (begins[TOK_DEV - 1] >= row_start).astype(jnp.float32)
        return local_state + (1.0 - flag) * summed_state, (lin_out, lin_dq)

    zero_state = jnp.zeros((HEADS, HD, HD), jnp.float32)
    _, (lin_out_b, lin_dq_b) = lax.scan(forward_step, zero_state, (query_b, key_b, value_b, grad_b, index_b, begin_b, block_ids))

    def backward_step(summed_state, inputs):
        query_rows, key_rows, value_rows, gradient_heads, ids, finishes, block = inputs
        row_end = (block + 1) * TOK_DEV
        lin_scores, lin_back = local_scores(query_rows, key_rows, value_rows, gradient_heads, ids)
        extended_rows = (finishes > row_end).astype(jnp.float32)[:, None, None]
        dk_inner = jnp.einsum('hts,thd->shd', lin_back.astype(jnp.float32), query_rows.astype(jnp.float32))
        outer_key_gradient = linear_scale * extended_rows * jnp.einsum('mdx,dwx->mdw', value_rows.astype(jnp.float32), summed_state, precision=highest_index)
        dv_inner = jnp.einsum('hts,thd->shd', lin_scores.astype(jnp.float32), gradient_heads.astype(jnp.float32))
        outer_value_gradient = linear_scale * extended_rows * jnp.einsum('nzt,zti->nzi', key_rows.astype(jnp.float32), summed_state, precision=highest_index)
        first_onehot = (ids == ids[0]).astype(jnp.float32)[:, None, None]
        local_state = jnp.einsum('cis,ciy->isy', query_rows.astype(jnp.float32) * first_onehot, gradient_heads.astype(jnp.float32))
        flag = (finishes[0] <= row_end).astype(jnp.float32)
        return local_state + (1.0 - flag) * summed_state, ((dk_inner + outer_key_gradient).astype(jnp.bfloat16), (dv_inner + outer_value_gradient).astype(jnp.bfloat16))

    _, (lin_dk_b, lin_dv_b) = lax.scan(backward_step, zero_state, (query_b, key_b, value_b, grad_b, index_b, finish_b, block_ids), reverse=True)

    pad_rows = REACH * TOK_DEV
    window_rows = (REACH + 1) * TOK_DEV
    key_pad = jnp.concatenate([jnp.zeros((pad_rows, feat_cols), jnp.bfloat16), soft_key], axis=0)
    value_pad = jnp.concatenate([jnp.zeros((pad_rows, feat_cols), jnp.bfloat16), soft_value], axis=0)
    soft_query_b = blocked(soft_query)

    def soft_step(grads_pad, inputs):
        query_rows, gradient_heads, ids, block = inputs
        row_start = (block * TOK_DEV).astype(jnp.int32)
        positions_q = row_start + order
        key_heads = lax.dynamic_slice_in_dim(key_pad, row_start, window_rows, 0).reshape(window_rows, HEADS, HD)
        value_heads = lax.dynamic_slice_in_dim(value_pad, row_start, window_rows, 0).reshape(window_rows, HEADS, HD)
        positions_k = (row_start - pad_rows + jnp.arange(window_rows, dtype=jnp.int32)).astype(jnp.int32)
        _, key_docs, _, _ = token_docs(doc_lengths, positions_k)
        allowed = (key_docs[None, :] == ids[:, None]) & (positions_k[None, :] <= positions_q[:, None]) & (positions_k[None, :] >= 0)
        scores = soft_scale * jnp.einsum('thd,shd->hts', query_rows.astype(jnp.float32), key_heads.astype(jnp.float32))
        scores = jnp.where(allowed[None], scores, -jnp.inf)
        row_max = jnp.max(scores, axis=2, keepdims=True)
        log_total = row_max + jnp.log(jnp.sum(jnp.exp(scores - row_max), axis=2, keepdims=True))
        soft_prob = jnp.exp(scores - log_total)
        soft_weights = soft_prob.astype(jnp.bfloat16)
        soft_out = jnp.einsum('hts,shd->thd', soft_weights.astype(jnp.float32), value_heads.astype(jnp.float32)).astype(jnp.bfloat16)
        delta = jnp.sum(gradient_heads.astype(jnp.float32) * soft_out.astype(jnp.float32), axis=2)
        grad_prob = jnp.einsum('thd,shd->hts', gradient_heads.astype(jnp.float32), value_heads.astype(jnp.float32))
        soft_ds = (soft_prob * (grad_prob - delta.T[:, :, None]) * soft_scale).astype(jnp.bfloat16)
        soft_dq = jnp.einsum('hts,shd->thd', soft_ds.astype(jnp.float32), key_heads.astype(jnp.float32)).astype(jnp.bfloat16)
        key_grad = jnp.einsum('hts,thd->shd', soft_ds.astype(jnp.float32), query_rows.astype(jnp.float32)).reshape(window_rows, feat_cols)
        value_grad = jnp.einsum('hts,thd->shd', soft_weights.astype(jnp.float32), gradient_heads.astype(jnp.float32)).reshape(window_rows, feat_cols)
        key_acc, value_acc = grads_pad
        key_acc = lax.dynamic_update_slice_in_dim(key_acc, lax.dynamic_slice_in_dim(key_acc, row_start, window_rows, 0) + key_grad, row_start, 0)
        value_acc = lax.dynamic_update_slice_in_dim(value_acc, lax.dynamic_slice_in_dim(value_acc, row_start, window_rows, 0) + value_grad, row_start, 0)
        return (key_acc, value_acc), (soft_out, soft_dq)

    zero_pad = jnp.zeros((SEQ + pad_rows, feat_cols), jnp.float32)
    (key_total, value_total), (soft_out_b, soft_dq_b) = lax.scan(soft_step, (zero_pad, zero_pad), (soft_query_b, grad_b, index_b, block_ids))

    lin_out = lin_out_b.reshape(SEQ, feat_cols)
    soft_out = soft_out_b.reshape(SEQ, feat_cols)
    contrib = weights * jnp.sum(upstream.astype(jnp.float32) * (lin_out.astype(jnp.float32) + soft_out.astype(jnp.float32)), axis=1)
    domain_loss = jnp.sum(contrib[:, None] * domain_hot, axis=0)
    return (lin_dq_b.reshape(SEQ, feat_cols), lin_dk_b.reshape(SEQ, feat_cols), lin_dv_b.reshape(SEQ, feat_cols),
            soft_dq_b.reshape(SEQ, feat_cols), key_total[pad_rows:].astype(jnp.bfloat16), value_total[pad_rows:].astype(jnp.bfloat16),
            domain_loss)
```

```python
import functools

import jax
import jax.numpy as jnp
from jax import lax
from jax.experimental import pallas as pl
from jax.experimental.pallas import tpu as pltpu
from jax.sharding import PartitionSpec as P

HD = 128
DOC_MOST = 384
NDOM = 8
LIN_SCALE = (HD * DOC_MOST) ** (-0.5)
SOFT_SCALE = HD ** (-0.5)
LOG2E = 1.4426950408889634
NEG = -1e30
HEADS_STEP = 4
VMEM = 40 * 1024 * 1024

F32 = jnp.float32
BF16 = jnp.bfloat16


def nn(a, b):
    return lax.dot_general(a, b, (((1,), (0,)), ((), ())), preferred_element_type=F32)


def nt(a, b):
    return lax.dot_general(a, b, (((1,), (1,)), ((), ())), preferred_element_type=F32)


def tn(a, b):
    return lax.dot_general(a, b, (((0,), (0,)), ((), ())), preferred_element_type=F32)


def iota(shape, dim):
    return lax.broadcasted_iota(jnp.int32, shape, dim).astype(F32)


def cols(h):
    return slice(h * HD, (h + 1) * HD)


def pack_kernel(lens, doms, wts, place, lq, lk, lv, sq, sk, sv, up, f_out, b_out, mr, mc):
    rows = lq.shape[0]

    @pl.when(pl.program_id(0) == 0)
    def _():
        first = place[0] * rows
        pos = first + lax.broadcasted_iota(jnp.int32, (1, HD), 1)

        def one(i, carry):
            start, begin, end, dom, wt = carry
            stop = start + lens[i]
            inside = (pos >= start) & (pos < stop)
            begin = jnp.where(inside, start.astype(F32), begin)
            end = jnp.where(inside, stop.astype(F32), end)
            dom = jnp.where(inside, doms[i].astype(F32), dom)
            wt = jnp.where(inside, wts[doms[i]], wt)
            return stop, begin, end, dom, wt

        zero = jnp.zeros((1, HD), F32)
        _, begin, end, dom, wt = lax.fori_loop(
            0, lens.shape[0], one, (jnp.int32(0), zero, zero, zero, zero)
        )
        mr[0:1, :] = begin
        mr[1:2, :] = end
        mr[2:3, :] = dom
        mr[3:4, :] = wt
        mr[4:8, :] = jnp.zeros((4, HD), F32)
        square = (rows, HD)
        mc[0:rows, :] = jnp.broadcast_to(begin, square).T
        mc[rows : 2 * rows, :] = jnp.broadcast_to(end, square).T
        mc[2 * rows : 3 * rows, :] = jnp.broadcast_to(wt, square).T

    begin_c = mc[0:rows, :]
    weight = mc[2 * rows : 3 * rows, :]
    in_last = (begin_c == begin_c[rows - 1 : rows, :]).astype(BF16)
    in_first = (begin_c == begin_c[0:1, :]).astype(BF16)
    f_out[0:rows, :] = sk[...]
    f_out[rows : 2 * rows, :] = sv[...]
    b_out[0:rows, :] = sq[...]
    for h in range(HEADS_STEP):
        c = cols(h)
        grad = (weight * up[:, c].astype(F32)).astype(BF16)
        b_out[rows : 2 * rows, c] = grad
        f_out[2 * rows : 3 * rows, c] = tn(lk[:, c] * in_last, lv[:, c]).astype(BF16)
        b_out[2 * rows : 3 * rows, c] = tn(lq[:, c] * in_first, grad).astype(BF16)


def query_kernel(place, mr, mc, f_own, b_own, lq, lk, lv, wr, wa, wx, sdq, ldq, stats, bias, cm, acc, soft):
    rows = lq.shape[0]
    step = pl.program_id(0)
    block = place[0]
    odd = block % 2
    offs = (2, jnp.where(odd == 1, 3, 1), jnp.where(odd == 1, 1, 3))
    square = (rows, HD)

    @pl.when(step == 0)
    def _():
        begin = mr[0:1, :]
        sub, lane = iota(square, 0), iota(square, 1)
        for i, o in enumerate(offs):
            pos = ((block - o) * rows).astype(F32) + sub
            bias[i * rows : (i + 1) * rows, :] = jnp.where(pos >= begin, 0.0, NEG)
        own = (block * rows).astype(F32) + sub
        bias[3 * rows : 4 * rows, :] = jnp.where((own >= begin) & (sub <= lane), 0.0, NEG)
        cm[...] = jnp.where((mc[0:rows, :] == begin) & (sub <= lane), LIN_SCALE, 0.0)
        acc[...] = jnp.zeros(square, F32)
        soft[...] = jnp.zeros((8, HD), F32)
        stats[...] = jnp.zeros_like(stats)

    begin_c = mc[0:rows, :]
    carried = jnp.where(begin_c < (block * rows).astype(F32), LIN_SCALE, 0.0)
    begin0 = begin_c[0:1, :]
    coef = [jnp.where(begin0 < ((block - o + 1) * rows).astype(F32), 1.0, 0.0) for o in offs]
    for h in range(HEADS_STEP):
        c = cols(h)
        q = b_own[0:rows, c]
        grad = b_own[rows : 2 * rows, c]
        keys = jnp.concatenate([wr[0:rows, c], wa[0:rows, c], wx[0:rows, c], f_own[0:rows, c]], axis=0)
        vals = jnp.concatenate(
            [w[rows : 2 * rows, c] for w in (wr, wa, wx, f_own)], axis=0
        )
        s = nt(keys, q) * (SOFT_SCALE * LOG2E) + bias[...]
        gp = nt(vals, grad)
        top = jnp.max(s, axis=0, keepdims=True)
        e = jnp.exp2(s - top)
        total = jnp.sum(e, axis=0, keepdims=True)
        prob = e * (1.0 / total)
        delta = jnp.sum(prob * gp, axis=0, keepdims=True)
        ds = (prob * (gp - delta) * SOFT_SCALE).astype(BF16)
        sdq[:, c] = tn(ds, keys).astype(BF16)
        row = step * HEADS_STEP + h
        stats[pl.ds(row, 1), :] = top + jnp.log2(total)
        stats[pl.ds(16 + row, 1), :] = delta
        soft[0:1, :] += delta
        prior = (
            coef[0] * wr[2 * rows : 3 * rows, c].astype(F32)
            + coef[1] * wa[2 * rows : 3 * rows, c].astype(F32)
            + coef[2] * wx[2 * rows : 3 * rows, c].astype(F32)
        ).astype(BF16)
        back = (cm[...] * nt(lv[:, c], grad)).astype(BF16)
        dq = tn(back, lk[:, c]) + carried * nt(grad, prior)
        ldq[:, c] = dq.astype(BF16)
        acc[...] += dq * lq[:, c].astype(F32)

    @pl.when(step == pl.num_programs(0) - 1)
    def _():
        r = jnp.sum(acc[...].T, axis=0, keepdims=True) + soft[0:1, :]
        stats[32:40, :] = jnp.where(mr[2:3, :] == iota((NDOM, HD), 0), r, 0.0)


def lin_key_kernel(place, mr, mc, b_own, lq, lk, lv, wr, wa, wx, ldk, ldv, cm):
    rows = lq.shape[0]
    block = place[0]
    odd = block % 2
    offs = (2, jnp.where(odd == 1, 1, 3), jnp.where(odd == 1, 3, 1))
    square = (rows, HD)

    @pl.when(pl.program_id(0) == 0)
    def _():
        sub, lane = iota(square, 0), iota(square, 1)
        cm[...] = jnp.where((mc[0:rows, :] == mr[0:1, :]) & (sub <= lane), LIN_SCALE, 0.0)

    end_c = mc[rows : 2 * rows, :]
    extended = jnp.where(end_c > ((block + 1) * rows).astype(F32), LIN_SCALE, 0.0)
    last = end_c[rows - 1 : rows, :]
    coef = [jnp.where(last > ((block + o) * rows).astype(F32), 1.0, 0.0) for o in offs]
    for h in range(HEADS_STEP):
        c = cols(h)
        grad = b_own[rows : 2 * rows, c]
        later = (
            coef[0] * wr[2 * rows : 3 * rows, c].astype(F32)
            + coef[1] * wa[2 * rows : 3 * rows, c].astype(F32)
            + coef[2] * wx[2 * rows : 3 * rows, c].astype(F32)
        ).astype(BF16)
        k, v, q = lk[:, c], lv[:, c], lq[:, c]
        scores = (cm[...] * nt(k, q)).astype(BF16)
        back = (cm[...] * nt(v, grad)).astype(BF16)
        ldk[:, c] = (nn(back, q) + extended * nt(v, later)).astype(BF16)
        ldv[:, c] = (nn(scores, grad) + extended * nn(k, later)).astype(BF16)


def soft_key_kernel(place, mc, f_own, b_own, wr, wa, wx, s0, s1, s2, s3, sdk, sdv, bias):
    rows = f_own.shape[0] // 3
    step = pl.program_id(0)
    block = place[0]
    odd = block % 2
    offs = (2, jnp.where(odd == 1, 1, 3), jnp.where(odd == 1, 3, 1))
    square = (rows, HD)

    @pl.when(step == 0)
    def _():
        end_c = mc[rows : 2 * rows, :]
        sub, lane = iota(square, 0), iota(square, 1)
        for i, o in enumerate(offs):
            pos = ((block + o) * rows).astype(F32) + lane
            bias[:, cols(i)] = jnp.where(pos < end_c, 0.0, NEG)
        own = (block * rows).astype(F32) + lane
        bias[:, cols(3)] = jnp.where((own < end_c) & (sub <= lane), 0.0, NEG)

    def stat(row):
        near, far = s1[pl.ds(row, 1), :], s3[pl.ds(row, 1), :]
        parts = [
            s2[pl.ds(row, 1), :],
            jnp.where(odd == 1, near, far),
            jnp.where(odd == 1, far, near),
            s0[pl.ds(row, 1), :],
        ]
        return jnp.concatenate(parts, axis=1)

    for h in range(HEADS_STEP):
        c = cols(h)
        k, v = f_own[0:rows, c], f_own[rows : 2 * rows, c]
        queries = jnp.concatenate([w[0:rows, c] for w in (wr, wa, wx, b_own)], axis=0)
        grads = jnp.concatenate([w[rows : 2 * rows, c] for w in (wr, wa, wx, b_own)], axis=0)
        row = step * HEADS_STEP + h
        s = nt(k, queries) * (SOFT_SCALE * LOG2E) + bias[...]
        prob = jnp.exp2(s - stat(row))
        gp = nt(v, grads)
        ds = (prob * (gp - stat(16 + row)) * SOFT_SCALE).astype(BF16)
        sdk[:, c] = nn(ds, queries).astype(BF16)
        sdv[:, c] = nn(prob.astype(BF16), grads).astype(BF16)


def on_device(lin_query, lin_key, lin_value, soft_query, soft_key, soft_value, upstream, doc_lengths, doc_domain, domain_weight):
    rows, feats = lin_query.shape
    wide = HEADS_STEP * HD
    steps = feats // wide
    count = lax.axis_size("ctx")
    block = lax.axis_index("ctx")
    place = block.astype(jnp.int32).reshape(1)

    smem = pl.BlockSpec(memory_space=pltpu.SMEM)

    def tall(n):
        return pl.BlockSpec((n * rows, wide), lambda i: (0, i))

    def whole(n):
        return pl.BlockSpec((n, HD), lambda i: (0, 0))

    params = pltpu.CompilerParams(dimension_semantics=("arbitrary",), vmem_limit_bytes=VMEM)
    one = jax.ShapeDtypeStruct((rows, feats), BF16)
    three = jax.ShapeDtypeStruct((3 * rows, feats), BF16)
    unit = rows * feats * 2
    mm = 2 * rows * HD * feats

    def call(kernel, name, in_specs, out_specs, out_shape, scratch, flops, traffic, *args):
        return pl.pallas_call(
            kernel,
            name=name,
            grid=(steps,),
            in_specs=in_specs,
            out_specs=out_specs,
            out_shape=out_shape,
            scratch_shapes=scratch,
            compiler_params=params,
            cost_estimate=pl.CostEstimate(flops=flops, bytes_accessed=traffic, transcendentals=0),
        )(*args)

    fwd, bwd, mr, mc = call(
        pack_kernel, "pack", [smem] * 4 + [tall(1)] * 7,
        [tall(3), tall(3), whole(8), whole(3 * rows)],
        [three, three, jax.ShapeDtypeStruct((8, HD), F32), jax.ShapeDtypeStruct((3 * rows, HD), F32)],
        [], 2 * mm, 13 * unit,
        doc_lengths, doc_domain, domain_weight, place,
        lin_query, lin_key, lin_value, soft_query, soft_key, soft_value, upstream,
    )

    def shift(x, by):
        return lax.ppermute(x, "ctx", [(i, i + by) for i in range(count) if 0 <= i + by < count])

    def around(x, by):
        return lax.ppermute(x, "ctx", [(i, (i + by) % count) for i in range(count)])

    def swap(x):
        return lax.ppermute(x, "ctx", [(i, i ^ 1) for i in range(count)])

    odd = block % 2 == 1
    fr = shift(fwd, 2)
    br = shift(bwd, -2)
    fa = swap(fr)
    fx = shift(jnp.where(odd, fr, fwd), 1)
    ba = swap(br)
    bx = shift(jnp.where(odd, bwd, br), -1)

    soft_dq, lin_dq, stats = call(
        query_kernel, "queries", [smem, whole(8), whole(3 * rows), tall(3), tall(3)] + [tall(1)] * 3 + [tall(3)] * 3,
        [tall(1), tall(1), whole(40)],
        [one, one, jax.ShapeDtypeStruct((40, HD), F32)],
        [pltpu.VMEM((4 * rows, HD), F32), pltpu.VMEM((rows, HD), F32), pltpu.VMEM((rows, HD), F32), pltpu.VMEM((8, HD), F32)],
        16 * mm, 20 * unit,
        place, mr, mc, fwd, bwd, lin_query, lin_key, lin_value, fr, fa, fx,
    )
    s1, s2, s3 = (around(stats, -o) for o in (1, 2, 3))

    lin_dk, lin_dv = call(
        lin_key_kernel, "lin_keys", [smem, whole(8), whole(3 * rows), tall(3)] + [tall(1)] * 3 + [tall(3)] * 3,
        [tall(1), tall(1)], [one, one], [pltpu.VMEM((rows, HD), F32)],
        6 * mm, 17 * unit,
        place, mr, mc, bwd, lin_query, lin_key, lin_value, br, ba, bx,
    )
    soft_dk, soft_dv = call(
        soft_key_kernel, "soft_keys", [smem, whole(3 * rows), tall(3), tall(3)] + [tall(3)] * 3 + [whole(40)] * 4,
        [tall(1), tall(1)], [one, one], [pltpu.VMEM((rows, 4 * HD), F32)],
        16 * mm, 17 * unit,
        place, mc, fwd, bwd, br, ba, bx, stats, s1, s2, s3,
    )

    loss = stats[32:40] + s1[32:40] + s2[32:40] + s3[32:40]
    for stride in (4, 16):
        loss = loss + sum(around(loss, stride * k) for k in (1, 2, 3))
    heads = lax.axis_size("head")
    loss = loss + sum(
        lax.ppermute(loss, "head", [(i, (i + k) % heads) for i in range(heads)]) for k in range(1, heads)
    )
    domain_loss = jnp.sum(loss, axis=1)
    return (lin_dq, lin_dk, lin_dv, soft_dq, soft_dk, soft_dv, domain_loss)


def solution(mesh):
    spec = P("ctx", "head")
    return jax.shard_map(
        on_device,
        mesh=mesh,
        in_specs=(spec,) * 7 + (P(),) * 3,
        out_specs=(spec,) * 6 + (P(),),
        check_vma=False,
    )
```

```python
import functools

import jax
import jax.numpy as jnp
from jax import lax
from jax.experimental import pallas as pl
from jax.experimental.pallas import tpu as pltpu
from jax.sharding import PartitionSpec as P

HD = 128
DOC_MOST = 384
NDOM = 8
LIN_SCALE = (HD * DOC_MOST) ** (-0.5)
SOFT_SCALE = HD ** (-0.5)
LOG2E = 1.4426950408889634
NEG = -1e30
HEADS_STEP = 4
PARTS = 1
RIDE = 4
QUERY_STEP = 4
VMEM = 16 * 1024 * 1024
PACK_VMEM = 60 * 1024 * 1024

F32 = jnp.float32
BF16 = jnp.bfloat16


def nn(a, b):
    return lax.dot_general(a, b, (((1,), (0,)), ((), ())), preferred_element_type=F32)


def nt(a, b):
    return lax.dot_general(a, b, (((1,), (1,)), ((), ())), preferred_element_type=F32)


def tn(a, b):
    return lax.dot_general(a, b, (((0,), (0,)), ((), ())), preferred_element_type=F32)


def iota(shape, dim):
    return lax.broadcasted_iota(jnp.int32, shape, dim).astype(F32)


def cols(h):
    return slice(h * HD, (h + 1) * HD)


def rows_kernel(lens, doms, wts, place, mr, mc):
    rows = mc.shape[0] // 4
    pos = place[0] * rows + lax.broadcasted_iota(jnp.int32, (1, HD), 1)
    begin = end = dom = wt = jnp.zeros((1, HD), F32)
    start = jnp.int32(0)
    for i in range(lens.shape[0]):
        stop = start + lens[i]
        inside = (pos >= start) & (pos < stop)
        begin = jnp.where(inside, start.astype(F32), begin)
        end = jnp.where(inside, stop.astype(F32), end)
        dom = jnp.where(inside, doms[i].astype(F32), dom)
        wt = jnp.where(inside, wts[doms[i]], wt)
        start = stop
    mr[0:1, :] = begin
    mr[1:2, :] = dom
    mr[2:8, :] = jnp.zeros((6, HD), F32)
    for i, row in enumerate((begin, end, dom, wt)):
        mc[i * rows : (i + 1) * rows, :] = jnp.broadcast_to(row, (rows, HD)).T


def pack_kernel(lens, doms, wts, place, lk, lv, sk, sv, lq, sq, up, f_out, b_out, mr, mc):
    rows = lk.shape[0]

    @pl.when(pl.program_id(0) == 0)
    def _():
        rows_kernel(lens, doms, wts, place, mr, mc)

    begin_c = mc[0:rows, :]
    weight = mc[3 * rows : 4 * rows, :]
    in_last = (begin_c == begin_c[rows - 1 : rows, :]).astype(BF16)
    in_first = (begin_c == begin_c[0:1, :]).astype(BF16)
    f_out[0:rows, :] = sk[...]
    f_out[rows : 2 * rows, :] = sv[...]
    b_out[0:rows, :] = sq[...]
    for h in range(QUERY_STEP):
        c = cols(h)
        f_out[2 * rows : 3 * rows, c] = tn(lk[:, c] * in_last, lv[:, c]).astype(BF16)
        grad = (weight * up[:, c].astype(F32)).astype(BF16)
        b_out[rows : 2 * rows, c] = grad
        b_out[2 * rows : 3 * rows, c] = tn(lq[:, c] * in_first, grad).astype(BF16)


def query_kernel(part, place, mr, mc, f_own, b_own, lq, lk, lv, wr, wa, wx, *rest):
    if part > 0:
        sdq_in, ldq_in, stats_in, acc_in, *rest = rest
    sdq, ldq, stats, acc_out, *rest = rest
    bias, cm, acc = rest[-3:]
    rows = lq.shape[0]
    step = pl.program_id(0)
    base = part * QUERY_STEP * pl.num_programs(0)
    block = place[0]
    offs = offsets(block % 2, True)
    square = (rows, HD)

    @pl.when(step == 0)
    def _():
        begin = mr[0:1, :]
        sub, lane = iota(square, 0), iota(square, 1)
        for i, o in enumerate(offs):
            pos = ((block - o) * rows).astype(F32) + sub
            bias[i * rows : (i + 1) * rows, :] = jnp.where(pos >= begin, 0.0, NEG)
        own = (block * rows).astype(F32) + sub
        bias[3 * rows : 4 * rows, :] = jnp.where((own >= begin) & (sub <= lane), 0.0, NEG)
        cm[...] = jnp.where((mc[0:rows, :] == begin) & (sub <= lane), LIN_SCALE, 0.0)
        if part > 0:
            acc[...] = acc_in[...]
            stats[...] = stats_in[...]
        else:
            acc[...] = jnp.zeros(square, F32)
            stats[...] = jnp.zeros_like(stats)

    begin_c = mc[0:rows, :]
    carried = jnp.where(begin_c < (block * rows).astype(F32), LIN_SCALE, 0.0)
    begin0 = begin_c[0:1, :]
    coef = [jnp.where(begin0 < ((block - o + 1) * rows).astype(F32), 1.0, 0.0) for o in offs]
    terms, deltas = [], []
    for h in range(QUERY_STEP):
        c = cols(h)
        q = b_own[0:rows, c]
        grad = b_own[rows : 2 * rows, c]
        keys = jnp.concatenate([w[0:rows, c] for w in (wr, wa, wx, f_own)], axis=0)
        vals = jnp.concatenate([w[rows : 2 * rows, c] for w in (wr, wa, wx, f_own)], axis=0)
        s = nt(keys, q) * (SOFT_SCALE * LOG2E) + bias[...]
        gp = nt(vals, grad)
        top = jnp.max(s, axis=0, keepdims=True)
        e = jnp.exp2(s - top)
        total = jnp.sum(e, axis=0, keepdims=True)
        prob = e * (1.0 / total)
        delta = jnp.sum(prob * gp, axis=0, keepdims=True)
        ds = (prob * (gp - delta) * SOFT_SCALE).astype(BF16)
        sdq[:, c] = tn(ds, keys).astype(BF16)
        row = base + step * QUERY_STEP + h
        stats[pl.ds(row, 1), :] = top + jnp.log2(total)
        stats[pl.ds(16 + row, 1), :] = delta
        deltas.append(delta)
        prior = sum(f * w[2 * rows : 3 * rows, c].astype(F32) for f, w in zip(coef, (wr, wa, wx))).astype(BF16)
        back = (cm[...] * nt(lv[:, c], grad)).astype(BF16)
        dq = tn(back, lk[:, c]) + carried * nt(grad, prior)
        ldq[:, c] = dq.astype(BF16)
        terms.append(dq * lq[:, c].astype(F32))
    diagonal = iota(square, 0) == iota(square, 1)
    acc[...] += sum(terms) + jnp.where(diagonal, sum(deltas), 0.0)

    @pl.when(step == pl.num_programs(0) - 1)
    def _():
        acc_out[...] = acc[...]
        if part == PARTS - 1:
            tokens = jnp.sum(acc[...], axis=1, keepdims=True)
            mine = jnp.where(mc[2 * rows : 3 * rows, :] == iota(square, 1), tokens, 0.0)
            vec = jnp.sum(mine, axis=0, keepdims=True)
            stats[32:40, :] = jnp.broadcast_to(vec, (8, HD))


def offsets(odd, forward):
    near, far = (3, 1) if forward else (1, 3)
    return 2, jnp.where(odd == 1, near, far), jnp.where(odd == 1, far, near)


def lin_key_kernel(place, mr, mc, b_own, lq, lk, lv, wr, wa, wx, ldk, ldv, cm):
    rows = lq.shape[0]
    block = place[0]
    odd = block % 2
    offs = offsets(odd, False)
    square = (rows, HD)

    @pl.when(pl.program_id(0) == 0)
    def _():
        sub, lane = iota(square, 0), iota(square, 1)
        cm[...] = jnp.where((mc[0:rows, :] == mr[0:1, :]) & (sub <= lane), LIN_SCALE, 0.0)

    end_c = mc[rows : 2 * rows, :]
    extended = jnp.where(end_c > ((block + 1) * rows).astype(F32), LIN_SCALE, 0.0)
    last = end_c[rows - 1 : rows, :]
    coef = [jnp.where(last > ((block + o) * rows).astype(F32), 1.0, 0.0) for o in offs]
    for h in range(HEADS_STEP):
        c = cols(h)
        grad = b_own[rows : 2 * rows, c]
        later = (
            coef[0] * wr[2 * rows : 3 * rows, c].astype(F32)
            + coef[1] * wa[2 * rows : 3 * rows, c].astype(F32)
            + coef[2] * wx[2 * rows : 3 * rows, c].astype(F32)
        ).astype(BF16)
        k, v, q = lk[:, c], lv[:, c], lq[:, c]
        scores = (cm[...] * nt(k, q)).astype(BF16)
        back = (cm[...] * nt(v, grad)).astype(BF16)
        ldk[:, c] = (nn(back, q) + extended * nt(v, later)).astype(BF16)
        ldv[:, c] = (nn(scores, grad) + extended * nn(k, later)).astype(BF16)


def soft_key_kernel(place, mc, k0, v0, b_own, wr, wa, wx, s0, s1, s2, s3, sdk, sdv, bias):
    rows = k0.shape[0]
    step = pl.program_id(0)
    block = place[0]
    odd = block % 2
    offs = offsets(odd, False)
    square = (rows, HD)

    @pl.when(step == 0)
    def _():
        end_c = mc[rows : 2 * rows, :]
        sub, lane = iota(square, 0), iota(square, 1)
        for i, o in enumerate(offs):
            pos = ((block + o) * rows).astype(F32) + lane
            bias[:, cols(i)] = jnp.where(pos < end_c, 0.0, NEG)
        own = (block * rows).astype(F32) + lane
        bias[:, cols(3)] = jnp.where((own < end_c) & (sub <= lane), 0.0, NEG)

    def stat(row):
        near, far = s1[pl.ds(row, 1), :], s3[pl.ds(row, 1), :]
        parts = [
            s2[pl.ds(row, 1), :],
            jnp.where(odd == 1, near, far),
            jnp.where(odd == 1, far, near),
            s0[pl.ds(row, 1), :],
        ]
        return jnp.concatenate(parts, axis=1)

    for h in range(HEADS_STEP):
        c = cols(h)
        k, v = k0[:, c], v0[:, c]
        queries = jnp.concatenate([w[0:rows, c] for w in (wr, wa, wx, b_own)], axis=0)
        grads = jnp.concatenate([w[rows : 2 * rows, c] for w in (wr, wa, wx, b_own)], axis=0)
        row = step * HEADS_STEP + h
        s = nt(k, queries) * (SOFT_SCALE * LOG2E) + bias[...]
        prob = jnp.exp2(s - stat(row))
        gp = nt(v, grads)
        ds = (prob * (gp - stat(16 + row)) * SOFT_SCALE).astype(BF16)
        sdk[:, c] = nn(ds, queries).astype(BF16)
        sdv[:, c] = nn(prob.astype(BF16), grads).astype(BF16)


def on_device(lin_query, lin_key, lin_value, soft_query, soft_key, soft_value, upstream, doc_lengths, doc_domain, domain_weight):
    rows, feats = lin_query.shape
    count, heads = lax.axis_size("ctx"), lax.axis_size("head")
    block = lax.axis_index("ctx")
    place = block.astype(jnp.int32).reshape(1)

    smem = pl.BlockSpec(memory_space=pltpu.SMEM)
    left = pl.BlockSpec(memory_space=pl.ANY)

    def tall(n, step=HEADS_STEP, first=0):
        return pl.BlockSpec((n * rows, step * HD), lambda i: (0, first + i))

    def whole(n):
        return pl.BlockSpec((n, HD), lambda i: (0, 0))

    def array(n, width=feats):
        return jax.ShapeDtypeStruct((n * rows, width), BF16)

    def small(n):
        return jax.ShapeDtypeStruct((n, HD), F32)

    unit = rows * feats * 2
    mm = 2 * rows * HD * feats

    def call(kernel, name, steps, in_specs, out_specs, out_shape, scratch, flops, traffic, args, vmem=VMEM, aliases=None):
        return pl.pallas_call(
            kernel,
            name=name,
            grid=(steps,),
            in_specs=in_specs,
            out_specs=out_specs,
            out_shape=out_shape,
            scratch_shapes=[pltpu.VMEM(s, F32) for s in scratch],
            input_output_aliases=aliases or {},
            compiler_params=pltpu.CompilerParams(dimension_semantics=("arbitrary",), vmem_limit_bytes=vmem),
            cost_estimate=pl.CostEstimate(flops=flops, bytes_accessed=traffic, transcendentals=0),
        )(*args)

    part_steps = feats // HD // PARTS // QUERY_STEP
    part_feats = feats // PARTS
    fwd, bwd, mr, mc = call(
        pack_kernel, "pack", PARTS * part_steps, [smem] * 4 + [tall(1, QUERY_STEP)] * 7,
        [tall(3, QUERY_STEP)] * 2 + [whole(8), whole(4 * rows)],
        [array(3)] * 2 + [small(8), small(4 * rows)],
        [], 2 * mm, 13 * unit,
        (doc_lengths, doc_domain, domain_weight, place,
         lin_key, lin_value, soft_key, soft_value, lin_query, soft_query, upstream),
        PACK_VMEM,
    )

    def shift(x, by):
        return lax.ppermute(x, "ctx", [(i, i + by) for i in range(count) if 0 <= i + by < count])

    def swap(x):
        return lax.ppermute(x, "ctx", [(i, i ^ 1) for i in range(count)])

    odd = block % 2 == 1

    fwd_first = shift(fwd, 2)
    bwd_first = shift(bwd, -2)

    def heads_of(x, p):
        return lax.slice_in_dim(x, p * part_feats, (p + 1) * part_feats, axis=1)

    fwd_far = [shift(jnp.where(odd, heads_of(fwd_first, p), heads_of(fwd, p)), 1) for p in range(PARTS)]
    fwd_swap = swap(fwd_first)
    bwds = bwd_first, swap(bwd_first), shift(jnp.where(odd, bwd, bwd_first), -1)

    results = ()
    for p in range(PARTS):
        one = tall(1, QUERY_STEP, p * part_steps)
        three = tall(3, QUERY_STEP, p * part_steps)
        held = tall(3, QUERY_STEP)
        fixed = 12
        results = call(
            functools.partial(query_kernel, p), "queries", part_steps,
            [smem, whole(8), whole(4 * rows), three, three] + [one] * 3 + [three, three, held]
            + ([left, left, whole(40), whole(rows)] if p > 0 else []),
            [one, one, whole(40), whole(rows)],
            [array(1), array(1), small(40), small(rows)],
            [(4 * rows, HD), (rows, HD), (rows, HD)],
            16 * mm // PARTS, 20 * unit // PARTS,
            (place, mr, mc, fwd, bwd, lin_query, lin_key, lin_value, fwd_first, fwd_swap, fwd_far[p], *results),
            aliases={fixed - 1: 0, fixed: 1} if p > 0 else None,
        )
    soft_dq, lin_dq, stats, _ = results
    s1, s2, s3 = (
        lax.ppermute(stats, "ctx", [(i, (i - o) % count) for i in range(count)]) for o in range(1, RIDE)
    )

    def lin_keys_side(*bwds):
        return call(
            lin_key_kernel, "lin_keys", feats // HD // HEADS_STEP,
            [smem, whole(8), whole(4 * rows), tall(3)] + [tall(1)] * 3 + [tall(3)] * 3,
            [tall(1), tall(1)], [array(1)] * 2, [(rows, HD)],
            6 * mm, 17 * unit,
            (place, mr, mc, bwd, lin_query, lin_key, lin_value, *bwds),
        )

    def soft_keys_side(*stats_rows):
        return call(
            soft_key_kernel, "soft_keys", feats // HD // HEADS_STEP,
            [smem, whole(4 * rows), tall(1), tall(1), tall(3)] + [tall(3)] * 3 + [whole(40)] * 4,
            [tall(1), tall(1)], [array(1)] * 2, [(rows, 4 * HD)],
            16 * mm, 17 * unit,
            (place, mc, soft_key, soft_value, bwd, *bwds, stats, *stats_rows),
        )

    slots = count // RIDE * heads
    groups = [[(g * RIDE + i) * heads + h for g in range(count // RIDE) for h in range(heads)] for i in range(RIDE)]
    lin_dk, lin_dv = lin_keys_side(*bwds)
    s1, s2, s3, lin_dk, lin_dv = lax.optimization_barrier((s1, s2, s3, lin_dk, lin_dv))
    vec = stats[32:33] + s1[32:33] + s2[32:33] + s3[32:33]
    vec, s1, s2, s3 = lax.optimization_barrier((vec, s1, s2, s3))
    got = lax.all_to_all(
        jnp.broadcast_to(vec, (slots, HD)), ("ctx", "head"), 0, 0, tiled=True, axis_index_groups=groups
    )
    soft_dk, soft_dv = soft_keys_side(s1, s2, s3)
    got, soft_dk, soft_dv = lax.optimization_barrier((got, soft_dk, soft_dv))
    domain_loss = jnp.sum(got, axis=0)[:NDOM]
    return (lin_dq, lin_dk, lin_dv, soft_dq, soft_dk, soft_dv, domain_loss)


def solution(mesh):
    spec = P("ctx", "head")
    return jax.shard_map(
        on_device,
        mesh=mesh,
        in_specs=(spec,) * 7 + (P(),) * 3,
        out_specs=(spec,) * 6 + (P(),),
        check_vma=False,
    )
```

```python
import functools

import jax
import jax.numpy as jnp
from jax import lax
from jax.experimental import pallas as pl
from jax.experimental.pallas import tpu as pltpu
from jax.sharding import PartitionSpec as P

HD = 128
DOC_MOST = 384
NDOM = 8
LIN_SCALE = (HD * DOC_MOST) ** (-0.5)
SOFT_SCALE = HD ** (-0.5)
LOG2E = 1.4426950408889634
NEG = -1e30
HEADS_STEP = 4
PARTS = 1
RIDE = 4
QUERY_STEP = 4
VMEM = 16 * 1024 * 1024
PACK_VMEM = 60 * 1024 * 1024

F32 = jnp.float32
BF16 = jnp.bfloat16


def nn(a, b):
    return lax.dot_general(a, b, (((1,), (0,)), ((), ())), preferred_element_type=F32)


def nt(a, b):
    return lax.dot_general(a, b, (((1,), (1,)), ((), ())), preferred_element_type=F32)


def tn(a, b):
    return lax.dot_general(a, b, (((0,), (0,)), ((), ())), preferred_element_type=F32)


def iota(shape, dim):
    return lax.broadcasted_iota(jnp.int32, shape, dim).astype(F32)


def cols(h):
    return slice(h * HD, (h + 1) * HD)


def rows_kernel(lens, doms, wts, place, mr, mc):
    rows = mc.shape[0] // 4
    pos = place[0] * rows + lax.broadcasted_iota(jnp.int32, (1, HD), 1)
    begin = end = dom = wt = jnp.zeros((1, HD), F32)
    start = jnp.int32(0)
    for i in range(lens.shape[0]):
        stop = start + lens[i]
        inside = (pos >= start) & (pos < stop)
        begin = jnp.where(inside, start.astype(F32), begin)
        end = jnp.where(inside, stop.astype(F32), end)
        dom = jnp.where(inside, doms[i].astype(F32), dom)
        wt = jnp.where(inside, wts[doms[i]], wt)
        start = stop
    mr[0:1, :] = begin
    mr[1:2, :] = dom
    mr[2:8, :] = jnp.zeros((6, HD), F32)
    for i, row in enumerate((begin, end, dom, wt)):
        mc[i * rows : (i + 1) * rows, :] = jnp.broadcast_to(row, (rows, HD)).T


def pack_forward_kernel(lens, doms, wts, place, lk, lv, sk, sv, f_out, mr, mc):
    rows = lk.shape[0]

    @pl.when(pl.program_id(0) == 0)
    def _():
        rows_kernel(lens, doms, wts, place, mr, mc)

    begin_c = mc[0:rows, :]
    in_last = (begin_c == begin_c[rows - 1 : rows, :]).astype(BF16)
    f_out[0:rows, :] = sk[...]
    f_out[rows : 2 * rows, :] = sv[...]
    for h in range(QUERY_STEP):
        c = cols(h)
        f_out[2 * rows : 3 * rows, c] = tn(lk[:, c] * in_last, lv[:, c]).astype(BF16)


def pack_backward_kernel(mc, lq, sq, up, b_out):
    rows = lq.shape[0]
    begin_c = mc[0:rows, :]
    weight = mc[3 * rows : 4 * rows, :]
    in_first = (begin_c == begin_c[0:1, :]).astype(BF16)
    b_out[0:rows, :] = sq[...]
    for h in range(QUERY_STEP):
        c = cols(h)
        grad = (weight * up[:, c].astype(F32)).astype(BF16)
        b_out[rows : 2 * rows, c] = grad
        b_out[2 * rows : 3 * rows, c] = tn(lq[:, c] * in_first, grad).astype(BF16)


def query_kernel(part, place, mr, mc, f_own, b_own, lq, inner, wr, wa, wx, *rest):
    if part > 0:
        sdq_in, ldq_in, stats_in, acc_in, *rest = rest
    sdq, ldq, stats, acc_out, *rest = rest
    bias, acc = rest[-2:]
    rows = lq.shape[0]
    step = pl.program_id(0)
    base = part * QUERY_STEP * pl.num_programs(0)
    block = place[0]
    offs = offsets(block % 2, True)
    square = (rows, HD)

    @pl.when(step == 0)
    def _():
        begin = mr[0:1, :]
        sub, lane = iota(square, 0), iota(square, 1)
        for i, o in enumerate(offs):
            pos = ((block - o) * rows).astype(F32) + sub
            bias[i * rows : (i + 1) * rows, :] = jnp.where(pos >= begin, 0.0, NEG)
        own = (block * rows).astype(F32) + sub
        bias[3 * rows : 4 * rows, :] = jnp.where((own >= begin) & (sub <= lane), 0.0, NEG)
        if part > 0:
            acc[...] = acc_in[...]
            stats[...] = stats_in[...]
        else:
            acc[...] = jnp.zeros(square, F32)
            stats[...] = jnp.zeros_like(stats)

    begin_c = mc[0:rows, :]
    carried = jnp.where(begin_c < (block * rows).astype(F32), LIN_SCALE, 0.0)
    begin0 = begin_c[0:1, :]
    coef = [jnp.where(begin0 < ((block - o + 1) * rows).astype(F32), 1.0, 0.0) for o in offs]
    terms, deltas = [], []
    for h in range(QUERY_STEP):
        c = cols(h)
        q = b_own[0:rows, c]
        grad = b_own[rows : 2 * rows, c]
        keys = jnp.concatenate([w[0:rows, c] for w in (wr, wa, wx, f_own)], axis=0)
        vals = jnp.concatenate([w[rows : 2 * rows, c] for w in (wr, wa, wx, f_own)], axis=0)
        s = nt(keys, q) * (SOFT_SCALE * LOG2E) + bias[...]
        gp = nt(vals, grad)
        top = jnp.max(s, axis=0, keepdims=True)
        e = jnp.exp2(s - top)
        total = jnp.sum(e, axis=0, keepdims=True)
        prob = e * (1.0 / total)
        delta = jnp.sum(prob * gp, axis=0, keepdims=True)
        ds = (prob * (gp - delta) * SOFT_SCALE).astype(BF16)
        sdq[:, c] = tn(ds, keys).astype(BF16)
        row = base + step * QUERY_STEP + h
        stats[pl.ds(row, 1), :] = top + jnp.log2(total)
        stats[pl.ds(16 + row, 1), :] = delta
        deltas.append(delta)
        prior = sum(f * w[2 * rows : 3 * rows, c].astype(F32) for f, w in zip(coef, (wr, wa, wx))).astype(BF16)
        dq = inner[:, c] + carried * nt(grad, prior)
        ldq[:, c] = dq.astype(BF16)
        terms.append(dq * lq[:, c].astype(F32))
    diagonal = iota(square, 0) == iota(square, 1)
    acc[...] += sum(terms) + jnp.where(diagonal, sum(deltas), 0.0)

    @pl.when(step == pl.num_programs(0) - 1)
    def _():
        acc_out[...] = acc[...]
        if part == PARTS - 1:
            tokens = jnp.sum(acc[...], axis=1, keepdims=True)
            mine = jnp.where(mc[2 * rows : 3 * rows, :] == iota(square, 1), tokens, 0.0)
            vec = jnp.sum(mine, axis=0, keepdims=True)
            stats[32:40, :] = jnp.broadcast_to(vec, (8, HD))


def offsets(odd, forward):
    near, far = (3, 1) if forward else (1, 3)
    return 2, jnp.where(odd == 1, near, far), jnp.where(odd == 1, far, near)


def inner_kernel(mr, mc, b_own, lq, lk, lv, dq, dk, dv, cm):
    rows = lq.shape[0]
    square = (rows, HD)

    @pl.when(pl.program_id(0) == 0)
    def _():
        sub, lane = iota(square, 0), iota(square, 1)
        cm[...] = jnp.where((mc[0:rows, :] == mr[0:1, :]) & (sub <= lane), LIN_SCALE, 0.0)

    for h in range(HEADS_STEP):
        c = cols(h)
        grad = b_own[rows : 2 * rows, c]
        k, q = lk[:, c], lq[:, c]
        scores = (cm[...] * nt(k, q)).astype(BF16)
        back = (cm[...] * nt(lv[:, c], grad)).astype(BF16)
        dq[:, c] = tn(back, k)
        dk[:, c] = nn(back, q)
        dv[:, c] = nn(scores, grad)


def lin_key_kernel(place, mc, lk, lv, dk, dv, wr, wa, wx, ldk, ldv):
    rows = lk.shape[0]
    block = place[0]
    end_c = mc[rows : 2 * rows, :]
    extended = jnp.where(end_c > ((block + 1) * rows).astype(F32), LIN_SCALE, 0.0)
    last = end_c[rows - 1 : rows, :]
    coef = [jnp.where(last > ((block + o) * rows).astype(F32), 1.0, 0.0) for o in offsets(block % 2, False)]
    for h in range(HEADS_STEP):
        c = cols(h)
        later = sum(f * w[:, c].astype(F32) for f, w in zip(coef, (wr, wa, wx))).astype(BF16)
        ldk[:, c] = (dk[:, c] + extended * nt(lv[:, c], later)).astype(BF16)
        ldv[:, c] = (dv[:, c] + extended * nn(lk[:, c], later)).astype(BF16)


def soft_key_kernel(place, mc, k0, v0, b_own, wr, wa, wx, s0, s1, s2, s3, sdk, sdv, bias):
    rows = k0.shape[0]
    step = pl.program_id(0)
    block = place[0]
    odd = block % 2
    offs = offsets(odd, False)
    square = (rows, HD)

    @pl.when(step == 0)
    def _():
        end_c = mc[rows : 2 * rows, :]
        sub, lane = iota(square, 0), iota(square, 1)
        for i, o in enumerate(offs):
            pos = ((block + o) * rows).astype(F32) + lane
            bias[:, cols(i)] = jnp.where(pos < end_c, 0.0, NEG)
        own = (block * rows).astype(F32) + lane
        bias[:, cols(3)] = jnp.where((own < end_c) & (sub <= lane), 0.0, NEG)

    def stat(row):
        near, far = s1[pl.ds(row, 1), :], s3[pl.ds(row, 1), :]
        parts = [
            s2[pl.ds(row, 1), :],
            jnp.where(odd == 1, near, far),
            jnp.where(odd == 1, far, near),
            s0[pl.ds(row, 1), :],
        ]
        return jnp.concatenate(parts, axis=1)

    for h in range(HEADS_STEP):
        c = cols(h)
        k, v = k0[:, c], v0[:, c]
        queries = jnp.concatenate([w[0:rows, c] for w in (wr, wa, wx, b_own)], axis=0)
        grads = jnp.concatenate([w[rows : 2 * rows, c] for w in (wr, wa, wx, b_own)], axis=0)
        row = step * HEADS_STEP + h
        s = nt(k, queries) * (SOFT_SCALE * LOG2E) + bias[...]
        prob = jnp.exp2(s - stat(row))
        gp = nt(v, grads)
        ds = (prob * (gp - stat(16 + row)) * SOFT_SCALE).astype(BF16)
        sdk[:, c] = nn(ds, queries).astype(BF16)
        sdv[:, c] = nn(prob.astype(BF16), grads).astype(BF16)


def on_device(lin_query, lin_key, lin_value, soft_query, soft_key, soft_value, upstream, doc_lengths, doc_domain, domain_weight):
    rows, feats = lin_query.shape
    count, heads = lax.axis_size("ctx"), lax.axis_size("head")
    block = lax.axis_index("ctx")
    place = block.astype(jnp.int32).reshape(1)

    smem = pl.BlockSpec(memory_space=pltpu.SMEM)
    left = pl.BlockSpec(memory_space=pl.ANY)

    def tall(n, step=HEADS_STEP, first=0):
        return pl.BlockSpec((n * rows, step * HD), lambda i: (0, first + i))

    def whole(n):
        return pl.BlockSpec((n, HD), lambda i: (0, 0))

    def array(n, width=feats):
        return jax.ShapeDtypeStruct((n * rows, width), BF16)

    def small(n):
        return jax.ShapeDtypeStruct((n, HD), F32)

    unit = rows * feats * 2
    mm = 2 * rows * HD * feats

    def call(kernel, name, steps, in_specs, out_specs, out_shape, scratch, flops, traffic, args, vmem=VMEM, aliases=None):
        return pl.pallas_call(
            kernel,
            name=name,
            grid=(steps,),
            in_specs=in_specs,
            out_specs=out_specs,
            out_shape=out_shape,
            scratch_shapes=[pltpu.VMEM(s, F32) for s in scratch],
            input_output_aliases=aliases or {},
            compiler_params=pltpu.CompilerParams(dimension_semantics=("arbitrary",), vmem_limit_bytes=vmem),
            cost_estimate=pl.CostEstimate(flops=flops, bytes_accessed=traffic, transcendentals=0),
        )(*args)

    part_steps = feats // HD // PARTS // QUERY_STEP
    part_feats = feats // PARTS
    fwd, mr, mc = call(
        pack_forward_kernel, "pack_forward", PARTS * part_steps, [smem] * 4 + [tall(1, QUERY_STEP)] * 4,
        [tall(3, QUERY_STEP), whole(8), whole(4 * rows)],
        [array(3), small(8), small(4 * rows)],
        [], mm, 7 * unit,
        (doc_lengths, doc_domain, domain_weight, place, lin_key, lin_value, soft_key, soft_value),
        PACK_VMEM,
    )
    (bwd,) = call(
        pack_backward_kernel, "pack_backward", PARTS * part_steps, [whole(4 * rows)] + [tall(1, QUERY_STEP)] * 3,
        [tall(3, QUERY_STEP)], [array(3)], [], mm, 6 * unit,
        (mc, lin_query, soft_query, upstream),
        PACK_VMEM,
    )

    def shift(x, by):
        return lax.ppermute(x, "ctx", [(i, i + by) for i in range(count) if 0 <= i + by < count])

    def swap(x):
        return lax.ppermute(x, "ctx", [(i, i ^ 1) for i in range(count)])

    odd = block % 2 == 1

    fwd_first = shift(fwd, 2)
    bwd_first = shift(bwd, -2)

    def heads_of(x, p):
        return lax.slice_in_dim(x, p * part_feats, (p + 1) * part_feats, axis=1)

    fwd_far = [shift(jnp.where(odd, heads_of(fwd_first, p), heads_of(fwd, p)), 1) for p in range(PARTS)]
    fwd_swap = swap(fwd_first)
    bwds = bwd_first, swap(bwd_first), shift(jnp.where(odd, bwd, bwd_first), -1)

    wide = jax.ShapeDtypeStruct((rows, feats), F32)
    dq_inner, dk_inner, dv_inner = call(
        inner_kernel, "inner", feats // HD // HEADS_STEP,
        [whole(8), whole(4 * rows), tall(3)] + [tall(1)] * 3, [tall(1)] * 3, [wide] * 3, [(rows, HD)],
        5 * mm, 12 * unit,
        (mr, mc, bwd, lin_query, lin_key, lin_value),
    )
    results = ()
    for p in range(PARTS):
        one = tall(1, QUERY_STEP, p * part_steps)
        three = tall(3, QUERY_STEP, p * part_steps)
        held = tall(3, QUERY_STEP)
        fixed = 12
        results = call(
            functools.partial(query_kernel, p), "queries", part_steps,
            [smem, whole(8), whole(4 * rows), three, three] + [one] * 2 + [three, three, held]
            + ([left, left, whole(40), whole(rows)] if p > 0 else []),
            [one, one, whole(40), whole(rows)],
            [array(1), array(1), small(40), small(rows)],
            [(4 * rows, HD), (rows, HD)],
            16 * mm // PARTS, 20 * unit // PARTS,
            (place, mr, mc, fwd, bwd, lin_query, dq_inner, fwd_first, fwd_swap, fwd_far[p], *results),
            aliases={fixed - 1: 0, fixed: 1} if p > 0 else None,
        )
    soft_dq, lin_dq, stats, _ = results
    s1, s2, s3 = (
        lax.ppermute(stats, "ctx", [(i, (i - o) % count) for i in range(count)]) for o in range(1, RIDE)
    )

    state = pl.BlockSpec((rows, HEADS_STEP * HD), lambda i: (2, i))

    def lin_keys_side(*bwds):
        return call(
            lin_key_kernel, "lin_keys", feats // HD // HEADS_STEP,
            [smem, whole(4 * rows)] + [tall(1)] * 4 + [state] * 3,
            [tall(1), tall(1)], [array(1)] * 2, [],
            2 * mm, 11 * unit,
            (place, mc, lin_key, lin_value, dk_inner, dv_inner, *bwds),
        )

    def soft_keys_side(*stats_rows):
        return call(
            soft_key_kernel, "soft_keys", feats // HD // HEADS_STEP,
            [smem, whole(4 * rows), tall(1), tall(1), tall(3)] + [tall(3)] * 3 + [whole(40)] * 4,
            [tall(1), tall(1)], [array(1)] * 2, [(rows, 4 * HD)],
            16 * mm, 17 * unit,
            (place, mc, soft_key, soft_value, bwd, *bwds, stats, *stats_rows),
        )

    slots = count // RIDE * heads
    groups = [[(g * RIDE + i) * heads + h for g in range(count // RIDE) for h in range(heads)] for i in range(RIDE)]
    lin_dk, lin_dv = lin_keys_side(*bwds)
    s1, s2, s3, lin_dk, lin_dv = lax.optimization_barrier((s1, s2, s3, lin_dk, lin_dv))
    vec = stats[32:33] + s1[32:33] + s2[32:33] + s3[32:33]
    vec, s1, s2, s3 = lax.optimization_barrier((vec, s1, s2, s3))
    got = lax.all_to_all(
        jnp.broadcast_to(vec, (slots, HD)), ("ctx", "head"), 0, 0, tiled=True, axis_index_groups=groups
    )
    soft_dk, soft_dv = soft_keys_side(s1, s2, s3)
    got, soft_dk, soft_dv = lax.optimization_barrier((got, soft_dk, soft_dv))
    domain_loss = jnp.sum(got, axis=0)[:NDOM]
    return (lin_dq, lin_dk, lin_dv, soft_dq, soft_dk, soft_dv, domain_loss)


def solution(mesh):
    spec = P("ctx", "head")
    return jax.shard_map(
        on_device,
        mesh=mesh,
        in_specs=(spec,) * 7 + (P(),) * 3,
        out_specs=(spec,) * 6 + (P(),),
        check_vma=False,
    )
```

```python
import functools

import jax
import jax.numpy as jnp
from jax import lax
from jax.experimental import pallas as pl
from jax.experimental.pallas import tpu as pltpu
from jax.sharding import PartitionSpec as P

HD = 128
DOC_MOST = 384
NDOM = 8
LIN_SCALE = (HD * DOC_MOST) ** (-0.5)
SOFT_SCALE = HD ** (-0.5)
LOG2E = 1.4426950408889634
NEG = -1e30
HEADS_STEP = 6
PARTS = 1
RIDE = 4
QUERY_STEP = 6
VMEM = 16 * 1024 * 1024
PACK_VMEM = 60 * 1024 * 1024

F32 = jnp.float32
BF16 = jnp.bfloat16


def nn(a, b):
    return lax.dot_general(a, b, (((1,), (0,)), ((), ())), preferred_element_type=F32)


def nt(a, b):
    return lax.dot_general(a, b, (((1,), (1,)), ((), ())), preferred_element_type=F32)


def tn(a, b):
    return lax.dot_general(a, b, (((0,), (0,)), ((), ())), preferred_element_type=F32)


def iota(shape, dim):
    return lax.broadcasted_iota(jnp.int32, shape, dim).astype(F32)


def cols(h):
    return slice(h * HD, (h + 1) * HD)


def rows_kernel(lens, doms, wts, place, mr, mc):
    rows = mc.shape[0] // 4
    pos = place[0] * rows + lax.broadcasted_iota(jnp.int32, (1, HD), 1)
    begin = end = dom = wt = jnp.zeros((1, HD), F32)
    start = jnp.int32(0)
    for i in range(lens.shape[0]):
        stop = start + lens[i]
        inside = (pos >= start) & (pos < stop)
        begin = jnp.where(inside, start.astype(F32), begin)
        end = jnp.where(inside, stop.astype(F32), end)
        dom = jnp.where(inside, doms[i].astype(F32), dom)
        wt = jnp.where(inside, wts[doms[i]], wt)
        start = stop
    mr[0:1, :] = begin
    mr[1:2, :] = dom
    mr[2:8, :] = jnp.zeros((6, HD), F32)
    for i, row in enumerate((begin, end, dom, wt)):
        mc[i * rows : (i + 1) * rows, :] = jnp.broadcast_to(row, (rows, HD)).T


def pack_forward_kernel(lens, doms, wts, place, lk, lv, sk, sv, f_out, mr, mc):
    rows = lk.shape[0]

    @pl.when(pl.program_id(0) == 0)
    def _():
        rows_kernel(lens, doms, wts, place, mr, mc)

    begin_c = mc[0:rows, :]
    in_last = (begin_c == begin_c[rows - 1 : rows, :]).astype(BF16)
    f_out[0:rows, :] = sk[...]
    f_out[rows : 2 * rows, :] = sv[...]
    for h in range(QUERY_STEP):
        c = cols(h)
        f_out[2 * rows : 3 * rows, c] = tn(lk[:, c] * in_last, lv[:, c]).astype(BF16)


def pack_backward_kernel(mc, lq, sq, up, b_out):
    rows = lq.shape[0]
    begin_c = mc[0:rows, :]
    weight = mc[3 * rows : 4 * rows, :]
    in_first = (begin_c == begin_c[0:1, :]).astype(BF16)
    b_out[0:rows, :] = sq[...]
    for h in range(QUERY_STEP):
        c = cols(h)
        grad = (weight * up[:, c].astype(F32)).astype(BF16)
        b_out[rows : 2 * rows, c] = grad
        b_out[2 * rows : 3 * rows, c] = tn(lq[:, c] * in_first, grad).astype(BF16)


def query_kernel(part, place, mr, mc, f_own, b_own, lq, inner, wr, wa, wx, *rest):
    if part > 0:
        sdq_in, ldq_in, stats_in, acc_in, *rest = rest
    sdq, ldq, stats, acc_out, *rest = rest
    bias, acc = rest[-2:]
    rows = lq.shape[0]
    step = pl.program_id(0)
    base = part * QUERY_STEP * pl.num_programs(0)
    block = place[0]
    offs = offsets(block % 2, True)
    square = (rows, HD)

    @pl.when(step == 0)
    def _():
        begin = mr[0:1, :]
        sub, lane = iota(square, 0), iota(square, 1)
        for i, o in enumerate(offs):
            pos = ((block - o) * rows).astype(F32) + sub
            bias[i * rows : (i + 1) * rows, :] = jnp.where(pos >= begin, 0.0, NEG)
        own = (block * rows).astype(F32) + sub
        bias[3 * rows : 4 * rows, :] = jnp.where((own >= begin) & (sub <= lane), 0.0, NEG)
        if part > 0:
            acc[...] = acc_in[...]
            stats[...] = stats_in[...]
        else:
            acc[...] = jnp.zeros(square, F32)
            stats[...] = jnp.zeros_like(stats)

    begin_c = mc[0:rows, :]
    carried = jnp.where(begin_c < (block * rows).astype(F32), LIN_SCALE, 0.0)
    begin0 = begin_c[0:1, :]
    coef = [jnp.where(begin0 < ((block - o + 1) * rows).astype(F32), 1.0, 0.0) for o in offs]
    terms, deltas = [], []
    for h in range(QUERY_STEP):
        c = cols(h)
        q = b_own[0:rows, c]
        grad = b_own[rows : 2 * rows, c]
        keys = jnp.concatenate([w[0:rows, c] for w in (wr, wa, wx, f_own)], axis=0)
        vals = jnp.concatenate([w[rows : 2 * rows, c] for w in (wr, wa, wx, f_own)], axis=0)
        s = nt(keys, q) * (SOFT_SCALE * LOG2E) + bias[...]
        gp = nt(vals, grad)
        top = jnp.max(s, axis=0, keepdims=True)
        e = jnp.exp2(s - top)
        total = jnp.sum(e, axis=0, keepdims=True)
        prob = e * (1.0 / total)
        delta = jnp.sum(prob * gp, axis=0, keepdims=True)
        ds = (prob * (gp - delta)).astype(BF16)
        sdq[:, c] = (tn(ds, keys) * SOFT_SCALE).astype(BF16)
        row = base + step * QUERY_STEP + h
        stats[pl.ds(row, 1), :] = top + jnp.log2(total)
        stats[pl.ds(16 + row, 1), :] = delta
        deltas.append(delta)
        prior = sum(f * w[2 * rows : 3 * rows, c].astype(F32) for f, w in zip(coef, (wr, wa, wx))).astype(BF16)
        dq = inner[:, c] + carried * nt(grad, prior)
        ldq[:, c] = dq.astype(BF16)
        terms.append(dq * lq[:, c].astype(F32))
    diagonal = iota(square, 0) == iota(square, 1)
    acc[...] += sum(terms) + jnp.where(diagonal, sum(deltas), 0.0)

    @pl.when(step == pl.num_programs(0) - 1)
    def _():
        acc_out[...] = acc[...]
        if part == PARTS - 1:
            tokens = jnp.sum(acc[...], axis=1, keepdims=True)
            mine = jnp.where(mc[2 * rows : 3 * rows, :] == iota(square, 1), tokens, 0.0)
            vec = jnp.sum(mine, axis=0, keepdims=True)
            stats[32:40, :] = jnp.broadcast_to(vec, (8, HD))


def offsets(odd, forward):
    near, far = (3, 1) if forward else (1, 3)
    return 2, jnp.where(odd == 1, near, far), jnp.where(odd == 1, far, near)


def inner_kernel(mr, mc, b_own, lq, lk, lv, dq, dk, dv, cm):
    rows = lq.shape[0]
    square = (rows, HD)

    @pl.when(pl.program_id(0) == 0)
    def _():
        sub, lane = iota(square, 0), iota(square, 1)
        cm[...] = jnp.where((mc[0:rows, :] == mr[0:1, :]) & (sub <= lane), LIN_SCALE, 0.0)

    for h in range(HEADS_STEP):
        c = cols(h)
        grad = b_own[rows : 2 * rows, c]
        k, q = lk[:, c], lq[:, c]
        scores = (cm[...] * nt(k, q)).astype(BF16)
        back = (cm[...] * nt(lv[:, c], grad)).astype(BF16)
        dq[:, c] = tn(back, k)
        dk[:, c] = nn(back, q)
        dv[:, c] = nn(scores, grad)


def lin_key_kernel(place, mc, lk, lv, dk, dv, wr, wa, wx, ldk, ldv):
    rows = lk.shape[0]
    block = place[0]
    end_c = mc[rows : 2 * rows, :]
    extended = jnp.where(end_c > ((block + 1) * rows).astype(F32), LIN_SCALE, 0.0)
    last = end_c[rows - 1 : rows, :]
    coef = [jnp.where(last > ((block + o) * rows).astype(F32), 1.0, 0.0) for o in offsets(block % 2, False)]
    for h in range(HEADS_STEP):
        c = cols(h)
        later = sum(f * w[:, c].astype(F32) for f, w in zip(coef, (wr, wa, wx))).astype(BF16)
        ldk[:, c] = (dk[:, c] + extended * nt(lv[:, c], later)).astype(BF16)
        ldv[:, c] = (dv[:, c] + extended * nn(lk[:, c], later)).astype(BF16)


def soft_key_kernel(place, mc, k0, v0, b_own, wr, wa, wx, s0, s1, s2, s3, sdk, sdv, bias):
    rows = k0.shape[0]
    step = pl.program_id(0)
    block = place[0]
    odd = block % 2
    offs = offsets(odd, False)
    square = (rows, HD)

    @pl.when(step == 0)
    def _():
        end_c = mc[rows : 2 * rows, :]
        sub, lane = iota(square, 0), iota(square, 1)
        for i, o in enumerate(offs):
            pos = ((block + o) * rows).astype(F32) + lane
            bias[:, cols(i)] = jnp.where(pos < end_c, 0.0, NEG)
        own = (block * rows).astype(F32) + lane
        bias[:, cols(3)] = jnp.where((own < end_c) & (sub <= lane), 0.0, NEG)

    def stat(row):
        near, far = s1[pl.ds(row, 1), :], s3[pl.ds(row, 1), :]
        parts = [
            s2[pl.ds(row, 1), :],
            jnp.where(odd == 1, near, far),
            jnp.where(odd == 1, far, near),
            s0[pl.ds(row, 1), :],
        ]
        return jnp.concatenate(parts, axis=1)

    for h in range(HEADS_STEP):
        c = cols(h)
        k, v = k0[:, c], v0[:, c]
        queries = jnp.concatenate([w[0:rows, c] for w in (wr, wa, wx, b_own)], axis=0)
        grads = jnp.concatenate([w[rows : 2 * rows, c] for w in (wr, wa, wx, b_own)], axis=0)
        row = step * HEADS_STEP + h
        s = nt(k, queries) * (SOFT_SCALE * LOG2E) + bias[...]
        prob = jnp.exp2(s - stat(row))
        gp = nt(v, grads)
        ds = (prob * (gp - stat(16 + row))).astype(BF16)
        sdk[:, c] = (nn(ds, queries) * SOFT_SCALE).astype(BF16)
        sdv[:, c] = nn(prob.astype(BF16), grads).astype(BF16)


def on_device(lin_query, lin_key, lin_value, soft_query, soft_key, soft_value, upstream, doc_lengths, doc_domain, domain_weight):
    rows, feats = lin_query.shape
    count, heads = lax.axis_size("ctx"), lax.axis_size("head")
    block = lax.axis_index("ctx")
    place = block.astype(jnp.int32).reshape(1)

    smem = pl.BlockSpec(memory_space=pltpu.SMEM)
    left = pl.BlockSpec(memory_space=pl.ANY)

    def tall(n, step=HEADS_STEP, first=0):
        return pl.BlockSpec((n * rows, step * HD), lambda i: (0, first + i))

    def whole(n):
        return pl.BlockSpec((n, HD), lambda i: (0, 0))

    def array(n, width=feats):
        return jax.ShapeDtypeStruct((n * rows, width), BF16)

    def small(n):
        return jax.ShapeDtypeStruct((n, HD), F32)

    unit = rows * feats * 2
    mm = 2 * rows * HD * feats

    def call(kernel, name, steps, in_specs, out_specs, out_shape, scratch, flops, traffic, args, vmem=VMEM, aliases=None):
        return pl.pallas_call(
            kernel,
            name=name,
            grid=(steps,),
            in_specs=in_specs,
            out_specs=out_specs,
            out_shape=out_shape,
            scratch_shapes=[pltpu.VMEM(s, F32) for s in scratch],
            input_output_aliases=aliases or {},
            compiler_params=pltpu.CompilerParams(dimension_semantics=("arbitrary",), vmem_limit_bytes=vmem),
            cost_estimate=pl.CostEstimate(flops=flops, bytes_accessed=traffic, transcendentals=0),
        )(*args)

    part_steps = feats // HD // PARTS // QUERY_STEP
    part_feats = feats // PARTS
    fwd, mr, mc = call(
        pack_forward_kernel, "pack_forward", PARTS * part_steps, [smem] * 4 + [tall(1, QUERY_STEP)] * 4,
        [tall(3, QUERY_STEP), whole(8), whole(4 * rows)],
        [array(3), small(8), small(4 * rows)],
        [], mm, 7 * unit,
        (doc_lengths, doc_domain, domain_weight, place, lin_key, lin_value, soft_key, soft_value),
        PACK_VMEM,
    )
    (bwd,) = call(
        pack_backward_kernel, "pack_backward", PARTS * part_steps, [whole(4 * rows)] + [tall(1, QUERY_STEP)] * 3,
        [tall(3, QUERY_STEP)], [array(3)], [], mm, 6 * unit,
        (mc, lin_query, soft_query, upstream),
        PACK_VMEM,
    )

    def shift(x, by):
        return lax.ppermute(x, "ctx", [(i, i + by) for i in range(count) if 0 <= i + by < count])

    def swap(x):
        return lax.ppermute(x, "ctx", [(i, i ^ 1) for i in range(count)])

    odd = block % 2 == 1

    fwd_first = shift(fwd, 2)
    bwd_first = shift(bwd, -2)

    def heads_of(x, p):
        return lax.slice_in_dim(x, p * part_feats, (p + 1) * part_feats, axis=1)

    fwd_far = [shift(jnp.where(odd, heads_of(fwd_first, p), heads_of(fwd, p)), 1) for p in range(PARTS)]
    fwd_swap = swap(fwd_first)
    bwds = bwd_first, swap(bwd_first), shift(jnp.where(odd, bwd, bwd_first), -1)

    wide = jax.ShapeDtypeStruct((rows, feats), F32)
    dq_inner, dk_inner, dv_inner = call(
        inner_kernel, "inner", feats // HD // HEADS_STEP,
        [whole(8), whole(4 * rows), tall(3)] + [tall(1)] * 3, [tall(1)] * 3, [wide] * 3, [(rows, HD)],
        5 * mm, 12 * unit,
        (mr, mc, bwd, lin_query, lin_key, lin_value),
    )
    results = ()
    for p in range(PARTS):
        one = tall(1, QUERY_STEP, p * part_steps)
        three = tall(3, QUERY_STEP, p * part_steps)
        held = tall(3, QUERY_STEP)
        fixed = 12
        results = call(
            functools.partial(query_kernel, p), "queries", part_steps,
            [smem, whole(8), whole(4 * rows), three, three] + [one] * 2 + [three, three, held]
            + ([left, left, whole(40), whole(rows)] if p > 0 else []),
            [one, one, whole(40), whole(rows)],
            [array(1), array(1), small(40), small(rows)],
            [(4 * rows, HD), (rows, HD)],
            16 * mm // PARTS, 20 * unit // PARTS,
            (place, mr, mc, fwd, bwd, lin_query, dq_inner, fwd_first, fwd_swap, fwd_far[p], *results),
            aliases={fixed - 1: 0, fixed: 1} if p > 0 else None,
        )
    soft_dq, lin_dq, stats, _ = results
    s1, s2, s3 = (
        lax.ppermute(stats, "ctx", [(i, (i - o) % count) for i in range(count)]) for o in range(1, RIDE)
    )

    state = pl.BlockSpec((rows, HEADS_STEP * HD), lambda i: (2, i))

    def lin_keys_side(*bwds):
        return call(
            lin_key_kernel, "lin_keys", feats // HD // HEADS_STEP,
            [smem, whole(4 * rows)] + [tall(1)] * 4 + [state] * 3,
            [tall(1), tall(1)], [array(1)] * 2, [],
            2 * mm, 11 * unit,
            (place, mc, lin_key, lin_value, dk_inner, dv_inner, *bwds),
        )

    def soft_keys_side(*stats_rows):
        return call(
            soft_key_kernel, "soft_keys", feats // HD // HEADS_STEP,
            [smem, whole(4 * rows), tall(1), tall(1), tall(3)] + [tall(3)] * 3 + [whole(40)] * 4,
            [tall(1), tall(1)], [array(1)] * 2, [(rows, 4 * HD)],
            16 * mm, 17 * unit,
            (place, mc, soft_key, soft_value, bwd, *bwds, stats, *stats_rows), PACK_VMEM,
        )

    slots = count // RIDE * heads
    groups = [[(g * RIDE + i) * heads + h for g in range(count // RIDE) for h in range(heads)] for i in range(RIDE)]
    lin_dk, lin_dv = lin_keys_side(*bwds)
    s1, s2, s3, lin_dk, lin_dv = lax.optimization_barrier((s1, s2, s3, lin_dk, lin_dv))
    vec = stats[32:33] + s1[32:33] + s2[32:33] + s3[32:33]
    vec, s1, s2, s3 = lax.optimization_barrier((vec, s1, s2, s3))
    got = lax.all_to_all(
        jnp.broadcast_to(vec, (slots, HD)), ("ctx", "head"), 0, 0, tiled=True, axis_index_groups=groups
    )
    soft_dk, soft_dv = soft_keys_side(s1, s2, s3)
    got, soft_dk, soft_dv = lax.optimization_barrier((got, soft_dk, soft_dv))
    domain_loss = jnp.sum(got, axis=0)[:NDOM]
    return (lin_dq, lin_dk, lin_dv, soft_dq, soft_dk, soft_dv, domain_loss)


def solution(mesh):
    spec = P("ctx", "head")
    return jax.shard_map(
        on_device,
        mesh=mesh,
        in_specs=(spec,) * 7 + (P(),) * 3,
        out_specs=(spec,) * 6 + (P(),),
        check_vma=False,
    )
```

```python
import functools

import jax
import jax.numpy as jnp
from jax import lax
from jax.experimental import pallas as pl
from jax.experimental.pallas import tpu as pltpu
from jax.sharding import PartitionSpec as P

HD = 128
DOC_MOST = 384
NDOM = 8
LIN_SCALE = (HD * DOC_MOST) ** (-0.5)
SOFT_SCALE = HD ** (-0.5)
LOG2E = 1.4426950408889634
NEG = -1e30
HEADS_STEP = 6
PARTS = 1
RIDE = 4
QUERY_STEP = 6
LIN_STEP = 12
VMEM = 16 * 1024 * 1024
PACK_VMEM = 60 * 1024 * 1024

F32 = jnp.float32
BF16 = jnp.bfloat16


def nn(a, b):
    return lax.dot_general(a, b, (((1,), (0,)), ((), ())), preferred_element_type=F32)


def nt(a, b):
    return lax.dot_general(a, b, (((1,), (1,)), ((), ())), preferred_element_type=F32)


def tn(a, b):
    return lax.dot_general(a, b, (((0,), (0,)), ((), ())), preferred_element_type=F32)


def iota(shape, dim):
    return lax.broadcasted_iota(jnp.int32, shape, dim).astype(F32)


def cols(h):
    return slice(h * HD, (h + 1) * HD)


def rows_kernel(lens, doms, wts, place, mr, mc):
    rows = mc.shape[0] // 4
    pos = place[0] * rows + lax.broadcasted_iota(jnp.int32, (1, HD), 1)
    begin = end = dom = wt = jnp.zeros((1, HD), F32)
    start = jnp.int32(0)
    for i in range(lens.shape[0]):
        stop = start + lens[i]
        inside = (pos >= start) & (pos < stop)
        begin = jnp.where(inside, start.astype(F32), begin)
        end = jnp.where(inside, stop.astype(F32), end)
        dom = jnp.where(inside, doms[i].astype(F32), dom)
        wt = jnp.where(inside, wts[doms[i]], wt)
        start = stop
    mr[0:1, :] = begin
    mr[1:2, :] = dom
    mr[2:8, :] = jnp.zeros((6, HD), F32)
    for i, row in enumerate((begin, end, dom, wt)):
        mc[i * rows : (i + 1) * rows, :] = jnp.broadcast_to(row, (rows, HD)).T


def pack_forward_kernel(lens, doms, wts, place, lk, lv, sk, sv, f_out, mr, mc):
    rows = lk.shape[0]

    @pl.when(pl.program_id(0) == 0)
    def _():
        rows_kernel(lens, doms, wts, place, mr, mc)

    begin_c = mc[0:rows, :]
    in_last = (begin_c == begin_c[rows - 1 : rows, :]).astype(BF16)
    f_out[0:rows, :] = sk[...]
    f_out[rows : 2 * rows, :] = sv[...]
    for h in range(QUERY_STEP):
        c = cols(h)
        f_out[2 * rows : 3 * rows, c] = tn(lk[:, c] * in_last, lv[:, c]).astype(BF16)


def pack_backward_kernel(mc, lq, sq, up, b_out):
    rows = lq.shape[0]
    begin_c = mc[0:rows, :]
    weight = mc[3 * rows : 4 * rows, :]
    in_first = (begin_c == begin_c[0:1, :]).astype(BF16)
    b_out[0:rows, :] = sq[...]
    for h in range(QUERY_STEP):
        c = cols(h)
        grad = (weight * up[:, c].astype(F32)).astype(BF16)
        b_out[rows : 2 * rows, c] = grad
        b_out[2 * rows : 3 * rows, c] = tn(lq[:, c] * in_first, grad).astype(BF16)


def query_kernel(part, place, mr, mc, f_own, b_own, lq, inner, wr, wa, wx, *rest):
    if part > 0:
        sdq_in, ldq_in, stats_in, acc_in, *rest = rest
    sdq, ldq, stats, acc_out, *rest = rest
    bias, acc = rest[-2:]
    rows = lq.shape[0]
    step = pl.program_id(0)
    base = part * QUERY_STEP * pl.num_programs(0)
    block = place[0]
    offs = offsets(block % 2, True)
    square = (rows, HD)

    @pl.when(step == 0)
    def _():
        begin = mr[0:1, :]
        sub, lane = iota(square, 0), iota(square, 1)
        for i, o in enumerate(offs):
            pos = ((block - o) * rows).astype(F32) + sub
            bias[i * rows : (i + 1) * rows, :] = jnp.where(pos >= begin, 0.0, NEG)
        own = (block * rows).astype(F32) + sub
        bias[3 * rows : 4 * rows, :] = jnp.where((own >= begin) & (sub <= lane), 0.0, NEG)
        if part > 0:
            acc[...] = acc_in[...]
            stats[...] = stats_in[...]
        else:
            acc[...] = jnp.zeros(square, F32)
            stats[...] = jnp.zeros_like(stats)

    begin_c = mc[0:rows, :]
    carried = jnp.where(begin_c < (block * rows).astype(F32), LIN_SCALE, 0.0)
    begin0 = begin_c[0:1, :]
    coef = [jnp.where(begin0 < ((block - o + 1) * rows).astype(F32), 1.0, 0.0) for o in offs]
    terms, deltas = [], []
    for h in range(QUERY_STEP):
        c = cols(h)
        q = b_own[0:rows, c]
        grad = b_own[rows : 2 * rows, c]
        keys = jnp.concatenate([w[0:rows, c] for w in (wr, wa, wx, f_own)], axis=0)
        vals = jnp.concatenate([w[rows : 2 * rows, c] for w in (wr, wa, wx, f_own)], axis=0)
        s = nt(keys, q) * (SOFT_SCALE * LOG2E) + bias[...]
        gp = nt(vals, grad)
        top = jnp.max(s, axis=0, keepdims=True)
        e = jnp.exp2(s - top)
        total = jnp.sum(e, axis=0, keepdims=True)
        prob = e * (1.0 / total)
        delta = jnp.sum(prob * gp, axis=0, keepdims=True)
        ds = (prob * (gp - delta)).astype(BF16)
        sdq[:, c] = (tn(ds, keys) * SOFT_SCALE).astype(BF16)
        row = base + step * QUERY_STEP + h
        stats[pl.ds(row, 1), :] = top + jnp.log2(total)
        stats[pl.ds(16 + row, 1), :] = delta
        deltas.append(delta)
        prior = sum(f * w[2 * rows : 3 * rows, c].astype(F32) for f, w in zip(coef, (wr, wa, wx))).astype(BF16)
        dq = inner[:, c] + carried * nt(grad, prior)
        ldq[:, c] = dq.astype(BF16)
        terms.append(dq * lq[:, c].astype(F32))
    diagonal = iota(square, 0) == iota(square, 1)
    acc[...] += sum(terms) + jnp.where(diagonal, sum(deltas), 0.0)

    @pl.when(step == pl.num_programs(0) - 1)
    def _():
        acc_out[...] = acc[...]
        if part == PARTS - 1:
            tokens = jnp.sum(acc[...], axis=1, keepdims=True)
            mine = jnp.where(mc[2 * rows : 3 * rows, :] == iota(square, 1), tokens, 0.0)
            vec = jnp.sum(mine, axis=0, keepdims=True)
            stats[32:40, :] = jnp.broadcast_to(vec, (8, HD))


def offsets(odd, forward):
    near, far = (3, 1) if forward else (1, 3)
    return 2, jnp.where(odd == 1, near, far), jnp.where(odd == 1, far, near)


def inner_kernel(mr, mc, b_own, lq, lk, lv, dq, dk, dv, cm):
    rows = lq.shape[0]
    square = (rows, HD)

    @pl.when(pl.program_id(0) == 0)
    def _():
        sub, lane = iota(square, 0), iota(square, 1)
        cm[...] = jnp.where((mc[0:rows, :] == mr[0:1, :]) & (sub <= lane), LIN_SCALE, 0.0)

    for h in range(LIN_STEP):
        c = cols(h)
        grad = b_own[rows : 2 * rows, c]
        k, q = lk[:, c], lq[:, c]
        scores = (cm[...] * nt(k, q)).astype(BF16)
        back = (cm[...] * nt(lv[:, c], grad)).astype(BF16)
        dq[:, c] = tn(back, k)
        dk[:, c] = nn(back, q)
        dv[:, c] = nn(scores, grad)


def lin_key_kernel(place, mc, lk, lv, dk, dv, wr, wa, wx, ldk, ldv):
    rows = lk.shape[0]
    block = place[0]
    end_c = mc[rows : 2 * rows, :]
    extended = jnp.where(end_c > ((block + 1) * rows).astype(F32), LIN_SCALE, 0.0)
    last = end_c[rows - 1 : rows, :]
    coef = [jnp.where(last > ((block + o) * rows).astype(F32), 1.0, 0.0) for o in offsets(block % 2, False)]
    for h in range(LIN_STEP):
        c = cols(h)
        later = sum(f * w[:, c].astype(F32) for f, w in zip(coef, (wr, wa, wx))).astype(BF16)
        ldk[:, c] = (dk[:, c] + extended * nt(lv[:, c], later)).astype(BF16)
        ldv[:, c] = (dv[:, c] + extended * nn(lk[:, c], later)).astype(BF16)


def soft_key_kernel(place, mc, k0, v0, b_own, wr, wa, wx, s0, s1, s2, s3, sdk, sdv, bias):
    rows = k0.shape[0]
    step = pl.program_id(0)
    block = place[0]
    odd = block % 2
    offs = offsets(odd, False)
    square = (rows, HD)

    @pl.when(step == 0)
    def _():
        end_c = mc[rows : 2 * rows, :]
        sub, lane = iota(square, 0), iota(square, 1)
        for i, o in enumerate(offs):
            pos = ((block + o) * rows).astype(F32) + lane
            bias[:, cols(i)] = jnp.where(pos < end_c, 0.0, NEG)
        own = (block * rows).astype(F32) + lane
        bias[:, cols(3)] = jnp.where((own < end_c) & (sub <= lane), 0.0, NEG)

    def stat(row):
        near, far = s1[pl.ds(row, 1), :], s3[pl.ds(row, 1), :]
        parts = [
            s2[pl.ds(row, 1), :],
            jnp.where(odd == 1, near, far),
            jnp.where(odd == 1, far, near),
            s0[pl.ds(row, 1), :],
        ]
        return jnp.concatenate(parts, axis=1)

    for h in range(HEADS_STEP):
        c = cols(h)
        k, v = k0[:, c], v0[:, c]
        queries = jnp.concatenate([w[0:rows, c] for w in (wr, wa, wx, b_own)], axis=0)
        grads = jnp.concatenate([w[rows : 2 * rows, c] for w in (wr, wa, wx, b_own)], axis=0)
        row = step * HEADS_STEP + h
        s = nt(k, queries) * (SOFT_SCALE * LOG2E) + bias[...]
        prob = jnp.exp2(s - stat(row))
        gp = nt(v, grads)
        ds = (prob * (gp - stat(16 + row))).astype(BF16)
        sdk[:, c] = (nn(ds, queries) * SOFT_SCALE).astype(BF16)
        sdv[:, c] = nn(prob.astype(BF16), grads).astype(BF16)


def on_device(lin_query, lin_key, lin_value, soft_query, soft_key, soft_value, upstream, doc_lengths, doc_domain, domain_weight):
    rows, feats = lin_query.shape
    count, heads = lax.axis_size("ctx"), lax.axis_size("head")
    block = lax.axis_index("ctx")
    place = block.astype(jnp.int32).reshape(1)

    smem = pl.BlockSpec(memory_space=pltpu.SMEM)
    left = pl.BlockSpec(memory_space=pl.ANY)

    def tall(n, step=HEADS_STEP, first=0):
        return pl.BlockSpec((n * rows, step * HD), lambda i: (0, first + i))

    def whole(n):
        return pl.BlockSpec((n, HD), lambda i: (0, 0))

    def array(n, width=feats):
        return jax.ShapeDtypeStruct((n * rows, width), BF16)

    def small(n):
        return jax.ShapeDtypeStruct((n, HD), F32)

    unit = rows * feats * 2
    mm = 2 * rows * HD * feats

    def call(kernel, name, steps, in_specs, out_specs, out_shape, scratch, flops, traffic, args, vmem=VMEM, aliases=None):
        return pl.pallas_call(
            kernel,
            name=name,
            grid=(steps,),
            in_specs=in_specs,
            out_specs=out_specs,
            out_shape=out_shape,
            scratch_shapes=[pltpu.VMEM(s, F32) for s in scratch],
            input_output_aliases=aliases or {},
            compiler_params=pltpu.CompilerParams(dimension_semantics=("arbitrary",), vmem_limit_bytes=vmem),
            cost_estimate=pl.CostEstimate(flops=flops, bytes_accessed=traffic, transcendentals=0),
        )(*args)

    part_steps = feats // HD // PARTS // QUERY_STEP
    part_feats = feats // PARTS
    fwd, mr, mc = call(
        pack_forward_kernel, "pack_forward", PARTS * part_steps, [smem] * 4 + [tall(1, QUERY_STEP)] * 4,
        [tall(3, QUERY_STEP), whole(8), whole(4 * rows)],
        [array(3), small(8), small(4 * rows)],
        [], mm, 7 * unit,
        (doc_lengths, doc_domain, domain_weight, place, lin_key, lin_value, soft_key, soft_value),
        PACK_VMEM,
    )
    (bwd,) = call(
        pack_backward_kernel, "pack_backward", PARTS * part_steps, [whole(4 * rows)] + [tall(1, QUERY_STEP)] * 3,
        [tall(3, QUERY_STEP)], [array(3)], [], mm, 6 * unit,
        (mc, lin_query, soft_query, upstream),
        PACK_VMEM,
    )

    def shift(x, by):
        return lax.ppermute(x, "ctx", [(i, i + by) for i in range(count) if 0 <= i + by < count])

    def swap(x):
        return lax.ppermute(x, "ctx", [(i, i ^ 1) for i in range(count)])

    odd = block % 2 == 1

    fwd_first = shift(fwd, 2)
    bwd_first = shift(bwd, -2)

    def heads_of(x, p):
        return lax.slice_in_dim(x, p * part_feats, (p + 1) * part_feats, axis=1)

    fwd_far = [shift(jnp.where(odd, heads_of(fwd_first, p), heads_of(fwd, p)), 1) for p in range(PARTS)]
    fwd_swap = swap(fwd_first)
    bwds = bwd_first, swap(bwd_first), shift(jnp.where(odd, bwd, bwd_first), -1)

    wide = jax.ShapeDtypeStruct((rows, feats), F32)
    dq_inner, dk_inner, dv_inner = call(
        inner_kernel, "inner", feats // HD // LIN_STEP,
        [whole(8), whole(4 * rows), tall(3, LIN_STEP)] + [tall(1, LIN_STEP)] * 3, [tall(1, LIN_STEP)] * 3, [wide] * 3, [(rows, HD)],
        5 * mm, 12 * unit,
        (mr, mc, bwd, lin_query, lin_key, lin_value),
    )
    results = ()
    for p in range(PARTS):
        one = tall(1, QUERY_STEP, p * part_steps)
        three = tall(3, QUERY_STEP, p * part_steps)
        held = tall(3, QUERY_STEP)
        fixed = 12
        results = call(
            functools.partial(query_kernel, p), "queries", part_steps,
            [smem, whole(8), whole(4 * rows), three, three] + [one] * 2 + [three, three, held]
            + ([left, left, whole(40), whole(rows)] if p > 0 else []),
            [one, one, whole(40), whole(rows)],
            [array(1), array(1), small(40), small(rows)],
            [(4 * rows, HD), (rows, HD)],
            16 * mm // PARTS, 20 * unit // PARTS,
            (place, mr, mc, fwd, bwd, lin_query, dq_inner, fwd_first, fwd_swap, fwd_far[p], *results),
            aliases={fixed - 1: 0, fixed: 1} if p > 0 else None,
        )
    soft_dq, lin_dq, stats, _ = results
    s1, s2, s3 = (
        lax.ppermute(stats, "ctx", [(i, (i - o) % count) for i in range(count)]) for o in range(1, RIDE)
    )

    state = pl.BlockSpec((rows, LIN_STEP * HD), lambda i: (2, i))

    def lin_keys_side(*bwds):
        return call(
            lin_key_kernel, "lin_keys", feats // HD // LIN_STEP,
            [smem, whole(4 * rows)] + [tall(1, LIN_STEP)] * 4 + [state] * 3,
            [tall(1, LIN_STEP), tall(1, LIN_STEP)], [array(1)] * 2, [],
            2 * mm, 11 * unit,
            (place, mc, lin_key, lin_value, dk_inner, dv_inner, *bwds),
        )

    def soft_keys_side(*stats_rows):
        return call(
            soft_key_kernel, "soft_keys", feats // HD // HEADS_STEP,
            [smem, whole(4 * rows), tall(1), tall(1), tall(3)] + [tall(3)] * 3 + [whole(40)] * 4,
            [tall(1), tall(1)], [array(1)] * 2, [(rows, 4 * HD)],
            16 * mm, 17 * unit,
            (place, mc, soft_key, soft_value, bwd, *bwds, stats, *stats_rows), PACK_VMEM,
        )

    slots = count // RIDE * heads
    groups = [[(g * RIDE + i) * heads + h for g in range(count // RIDE) for h in range(heads)] for i in range(RIDE)]
    lin_dk, lin_dv = lin_keys_side(*bwds)
    s1, s2, s3, lin_dk, lin_dv = lax.optimization_barrier((s1, s2, s3, lin_dk, lin_dv))
    vec = stats[32:33] + s1[32:33] + s2[32:33] + s3[32:33]
    vec, s1, s2, s3 = lax.optimization_barrier((vec, s1, s2, s3))
    got = lax.all_to_all(
        jnp.broadcast_to(vec, (slots, HD)), ("ctx", "head"), 0, 0, tiled=True, axis_index_groups=groups
    )
    soft_dk, soft_dv = soft_keys_side(s1, s2, s3)
    got, soft_dk, soft_dv = lax.optimization_barrier((got, soft_dk, soft_dv))
    domain_loss = jnp.sum(got, axis=0)[:NDOM]
    return (lin_dq, lin_dk, lin_dv, soft_dq, soft_dk, soft_dv, domain_loss)


def solution(mesh):
    spec = P("ctx", "head")
    return jax.shard_map(
        on_device,
        mesh=mesh,
        in_specs=(spec,) * 7 + (P(),) * 3,
        out_specs=(spec,) * 6 + (P(),),
        check_vma=False,
    )
```
